256 devices in a mesh: seq: 16 (over y, x), head: 16 (over z, core).
Axes of the slice: x: 4, y: 4, z: 8, core: 2. Of those that a mesh axis runs over, the one named last changes fastest.
Arguments:
- queries: bfloat16 [8192, 2048], P('seq', 'head'), may hold values from -5 to 5
- keys: bfloat16 [8192, 2048], P('seq', 'head'), may hold values from -5 to 5
- values: bfloat16 [8192, 2048], P('seq', 'head'), may hold values from -5 to 5
- grad_out: bfloat16 [8192, 2048], P('seq', 'head'), may hold values from -6 to 6
Outputs:
- attended: bfloat16 [8192, 2048], P('seq', 'head')
- grad_query: bfloat16 [8192, 2048], P(('seq', 'head'))
- grad_key: bfloat16 [8192, 2048], P(('seq', 'head'))
- grad_value: bfloat16 [8192, 2048], P(('seq', 'head'))
The draws below stay inside these ranges and needn't reach their ends.
All inputs are finite; a program needn't handle non-finite values.
Results may differ from the reference program's by a relative error of at most 0.024.
Values may be sent and summed in bfloat16 or wider, within the bound.
A program may use at most 64 MiB of HBM per device.

```python
from functools import reduce
import jax
import jax.numpy as jnp
from jax import lax

HEAD_DIM = 128
BLOCK = 128
HEADS = 16
WIDTH = 2048
TOKENS = 8192


def region_means(key):
    means = jax.random.normal(key, (64, WIDTH), jnp.float32)
    return jnp.repeat(means, TOKENS // 64, axis=0)


def rough_rows(key, salt):
    return jax.random.normal(jax.random.fold_in(key, salt), (TOKENS, WIDTH), jnp.float32)


def draw_queries(key, part):
    base = jnp.clip(rough_rows(key, 1) + region_means(jax.random.fold_in(key, 2)), -5.0, 5.0)
    return base.astype(jnp.bfloat16)


def draw_keys(key, part):
    base = jnp.clip(rough_rows(key, 11) + region_means(jax.random.fold_in(key, 12)), -5.0, 5.0)
    return base.astype(jnp.bfloat16)


def draw_values(key, part):
    return jnp.clip(rough_rows(key, 21) + region_means(jax.random.fold_in(key, 22)), -5.0, 5.0).astype(jnp.bfloat16)


def level_of(key, shape, shards, least, top_value):
    gain = 1.0
    for position, shards_of in shards:
        heights = jax.random.uniform(jax.random.fold_in(jax.random.fold_in(key, 6), position), (shards_of,), jnp.float32, least / len(shards), top_value / len(shards))
        gain = gain * jnp.repeat(jnp.exp(heights), shape[position] // shards_of).reshape((-1,) + (1,) * (len(shape) - 1 - position))
    return gain


def bell_draw(stream_key, shape, width, bound, split=(), kind=jnp.bfloat16):
    drawn = width * jax.random.normal(stream_key, shape, jnp.float32)
    if split:
        drawn = drawn * level_of(stream_key, shape, split, -0.22, 0.18)
    return jnp.clip(drawn, -bound, bound).astype(kind)


def setup_inputs(seed: int = 0) -> dict:
    arg_keys = jax.random.split(jax.random.key(seed), 5)
    return {
        "queries": draw_queries(jax.random.fold_in(arg_keys[4], 71), 0),
        "keys": draw_keys(jax.random.fold_in(arg_keys[4], 71), 0),
        "values": draw_values(jax.random.fold_in(arg_keys[4], 71), 0),
        "grad_out": bell_draw(arg_keys[3], (TOKENS, WIDTH), 1.0, 6.0, ((0, 16), (1, 16))),
    }


MASKED = -1e+30

def coarsen(stacked):
    in_shape = stacked.shape
    paired = stacked.astype(jnp.float32).reshape(in_shape[:-2] + (in_shape[-2] // 2, 2, in_shape[-1]))
    halved = ((paired[..., 0, :] + paired[..., 1, :]) * 0.5).astype(jnp.bfloat16)
    return lax.optimization_barrier(halved)

def unit_stats(query_rows, query_index, key_rows, value_rows, key_index, block_count, coarse_level, block_rows):
    scale = query_rows.shape[-1] ** (-0.5)
    scores = jnp.einsum('urd,ukd->urk', query_rows.astype(jnp.float32), key_rows.astype(jnp.float32)) * scale
    row_block = query_index // block_rows
    key_block = key_index // block_rows
    block_gap = jnp.abs(row_block[:, :, None] - key_block[:, None, :])
    if coarse_level == 0:
        allowed = block_gap <= 1
    else:
        parent_gap = jnp.abs(row_block[:, :, None] // 2 - key_block[:, None, :] // 2)
        allowed = (block_gap >= 2) & (parent_gap <= 1)
    allowed = allowed & (key_block[:, None, :] >= 0) & (key_block[:, None, :] < block_count)
    scores = jnp.where(allowed, scores, MASKED)
    row_peak = lax.optimization_barrier(jnp.max(scores, axis=-1))
    exp_scores = jnp.exp(scores - row_peak[..., None])
    multiple = float(2 ** coarse_level)
    row_total = lax.optimization_barrier(jnp.sum(exp_scores, axis=-1)) * multiple
    rounded = lax.optimization_barrier(exp_scores.astype(jnp.bfloat16))
    mixed_rows = jnp.einsum('urk,ukd->urd', rounded.astype(jnp.float32), value_rows.astype(jnp.float32)) * multiple
    return (row_peak, row_total, mixed_rows)

def windowed(coarse_query, padded, first_row, span_rows, block_count, coarse_level, block_rows):
    row_count, head_width = coarse_query.shape
    unit_count = row_count // span_rows
    unit_rows = padded.reshape(2, unit_count + 2, span_rows, head_width)
    window = jnp.concatenate([unit_rows[:, :-2], unit_rows[:, 1:-1], unit_rows[:, 2:]], axis=2)
    query_index = (first_row + jnp.arange(row_count, dtype=jnp.int32)).reshape(unit_count, span_rows)
    key_index = first_row - span_rows + jnp.arange(unit_count, dtype=jnp.int32)[:, None] * span_rows + jnp.arange(3 * span_rows, dtype=jnp.int32)[None, :]
    return unit_stats(coarse_query.reshape(unit_count, span_rows, head_width), query_index, window[0], window[1], key_index, block_count, coarse_level, block_rows)

def expand(stats, coarse_level, head_width):
    repeats = 2 ** coarse_level
    return (jnp.repeat(stats[0].reshape(-1), repeats), jnp.repeat(stats[1].reshape(-1), repeats), jnp.repeat(stats[2].reshape(-1, head_width), repeats, axis=0))

def combine(level_stats):
    overall_peak = reduce(jnp.maximum, [entry[0] for entry in level_stats])
    factors = [jnp.exp(entry[0] - overall_peak) for entry in level_stats]
    denominator = reduce(jnp.add, [factor * entry[1] for factor, entry in zip(factors, level_stats)])
    numerator = reduce(jnp.add, [factor[:, None] * entry[2] for factor, entry in zip(factors, level_stats)])
    return (numerator / denominator[:, None]).astype(jnp.bfloat16)

def attend_head(query_rows, key_rows, value_rows):
    token_count, head_width = query_rows.shape
    fine_blocks = token_count // BLOCK
    top_level = (fine_blocks // 4).bit_length() - 1
    key_value = jnp.stack([key_rows, value_rows])
    coarse_query = query_rows
    level_stats = []
    for coarse_level in range(top_level + 1):
        span_rows = BLOCK if coarse_level == 0 else 2 * BLOCK
        if coarse_level > 0:
            coarse_query = coarsen(coarse_query)
            key_value = coarsen(key_value)
        padded = jnp.pad(key_value, ((0, 0), (span_rows, span_rows), (0, 0)))
        stats = windowed(coarse_query, padded, 0, span_rows, fine_blocks >> coarse_level, coarse_level, BLOCK)
        level_stats.append(expand(stats, coarse_level, head_width))
    return combine(level_stats)

def one_head(inputs):
    query_rows, key_rows, value_rows, cotangent = inputs
    attended, pullback = jax.vjp(attend_head, query_rows, key_rows, value_rows)
    grad_query, grad_key, grad_value = pullback(cotangent)
    return (attended, grad_query, grad_key, grad_value)

def reference(queries, keys, values, grad_out):

    def by_head(matrix):
        return matrix.reshape(TOKENS, HEADS, HEAD_DIM).transpose(1, 0, 2)

    def from_head(stacked):
        return stacked.transpose(1, 0, 2).reshape(TOKENS, WIDTH)
    results = lax.map(one_head, (by_head(queries), by_head(keys), by_head(values), by_head(grad_out)))
    return (from_head(results[0]), from_head(results[1]), from_head(results[2]), from_head(results[3]))
```

```python
import functools

import jax
import jax.numpy as jnp
from jax import lax
from jax.experimental import pallas as pl
from jax.experimental.pallas import tpu as pltpu
from jax.sharding import PartitionSpec as P

BLOCK = 128
WIDE = 256
NEG = -1e30
F32 = jnp.float32
BF16 = jnp.bfloat16
LOG2E = 1.4426950408889634
MESH = pl.DeviceIdType.MESH
OFF = (0, 512, 768, 896, 960)
STACK = 992
SEM = (0, 2, 4, 7, 13)
SLOTS = 21
ROWS = (128, 256, 128, 64, 32)
SLOT_COUNT = (2, 2, 3, 6, 8)

NN = (((1,), (0,)), ((), ()))
NT = (((1,), (1,)), ((), ()))
TN = (((0,), (0,)), ((), ()))


def dot(a, b, dims=NN):
    return lax.dot_general(a, b, dims, preferred_element_type=F32)


def halve(x):
    n, w = x.shape
    x = x.reshape(n // 16, 2, 8, w)
    m = (x[:, 0] + x[:, 1]) * 0.5
    return m.astype(BF16).astype(F32).reshape(n // 2, w)


def expand(x, level):
    n, w = x.shape
    if level == 0:
        return x
    x = x.reshape(n // 8, 1, 8, w)
    x = jnp.broadcast_to(x, (n // 8, 1 << level, 8, w))
    return x.reshape(n << level, w)


def group(x, level):
    n, w = x.shape
    if level == 0:
        return x
    return x.reshape(n >> (level + 3), 1 << level, 8, w).sum(axis=1).reshape(n >> level, w)


def peers_of(s, seq_count):
    out = []
    prev, after = lax.rem(s + seq_count - 1, seq_count), lax.rem(s + 1, seq_count)
    a, e = lax.div(s, 2), lax.rem(s, 2)
    y, x = lax.div(s, 4), lax.rem(s, 4)

    def third(i, n):
        return lax.rem(i + n + 3 - 6 * lax.rem(i, 2), n)

    blocks = seq_count // 2
    for f in range(4):
        out.append((4, lax.rem(y + 2, 4) * 4 + f, f, x))
    for f in range(4):
        out.append((4, (3 - y) * 4 + f, 4 + f, 4 + x))
    far3 = third(a, blocks)
    for f in range(2):
        out.append((3, far3 * 2 + f, 4 + f, 4 + e))
    for f in range(2):
        out.append((3, lax.rem(a + blocks - 2, blocks) * 2 + f, f, 2 + e))
        out.append((3, lax.rem(a + 2, blocks) * 2 + f, 2 + f, e))
    out.append((2, third(s, seq_count), 2, 2))
    out.append((2, lax.rem(s + seq_count - 2, seq_count), 0, 1))
    out.append((2, lax.rem(s + 2, seq_count), 1, 0))
    out.append((1, prev, 0, 1))
    out.append((1, after, 1, 0))
    out.append((0, prev, 0, 1))
    out.append((0, after, 1, 0))
    return out


def kernel(
    seq_count, head_count,
    q_ref, k_ref, v_ref, g_ref,
    att_ref, gq_ref, gk_ref, gv_ref,
    kv0, kv1, kv2, kv3, kv4, in1, in2, in3, in4,
    qs, go, ee, pk, tot, sm, gg, dd, dq,
    acc0, acc1, bk0, bk1, bk2, bk3, bk4, rx0, rx1, rx2, rx3, rx4,
    oq, ok, ov,
    send_sem, recv_sem, back_send, back_recv, out_send, out_recv,
):
    s, h = lax.axis_index("seq"), lax.axis_index("head")
    barrier = pltpu.get_barrier_semaphore()
    for j in range(1, seq_count):
        pl.semaphore_signal(
            barrier, inc=1, device_id={"seq": lax.rem(s + j, seq_count)}, device_id_type=MESH
        )
    for j in range(1, head_count):
        pl.semaphore_signal(
            barrier, inc=1, device_id={"head": lax.rem(h + j, head_count)}, device_id_type=MESH
        )

    row = lax.broadcasted_iota(jnp.int32, (BLOCK, BLOCK), 0)
    col = lax.broadcasted_iota(jnp.int32, (BLOCK, BLOCK), 1)
    perm = jnp.where(col == (row & 7) * 16 + (row >> 3), 1.0, 0.0).astype(BF16)
    unperm = jnp.where(col == (row & 15) * 8 + (row >> 4), 1.0, 0.0).astype(BF16)

    own = (kv0, kv1, kv2, kv3, kv4)
    tops = []
    for b in range(4):
        rows = pl.ds(BLOCK * b, BLOCK)
        fine = dot(perm, jnp.concatenate([k_ref[rows, :], v_ref[rows, :]], axis=1))
        kv0[pl.ds(BLOCK + BLOCK * b, BLOCK), :] = fine.astype(BF16)
        m1 = halve(fine)
        kv1[pl.ds(64 * ((b + 2) % 4), 64), :] = m1.astype(BF16)
        m2 = halve(m1)
        kv2[pl.ds(32 * b, 32), :] = m2.astype(BF16)
        m3 = halve(m2)
        kv3[pl.ds(16 * b, 16), :] = m3.astype(BF16)
        tops.append(halve(m3))
    kv4[...] = jnp.concatenate(tops, axis=0).astype(BF16)

    pl.semaphore_wait(barrier, seq_count - 1 + head_count - 1)

    peers = peers_of(s, seq_count)
    inbox = (kv0, in1, in2, in3, in4)
    outbox = (bk0, bk1, bk2, bk3, bk4)
    rxbox = (rx0, rx1, rx2, rx3, rx4)

    def at_slot(ref, level, slot, spread=False):
        n = ROWS[level]
        if spread:
            return ref.at[pl.ds(640 * slot, n), :]
        return ref.at[pl.ds(n * slot, n), :]

    def forward_copy(entry):
        level, peer, slot, there = entry
        if level == 0:
            src = kv0.at[pl.ds(BLOCK + 384 * slot, BLOCK), :]
        else:
            src = own[level]
        return pltpu.make_async_remote_copy(
            src_ref=src,
            dst_ref=at_slot(inbox[level], level, there, level == 0),
            send_sem=send_sem.at[SEM[level] + slot],
            recv_sem=recv_sem.at[SEM[level] + there],
            device_id={"seq": peer},
            device_id_type=MESH,
        )

    def forward_arrival(level, slot):
        here = at_slot(inbox[level], level, slot, level == 0)
        pltpu.make_async_remote_copy(
            src_ref=here, dst_ref=here,
            send_sem=send_sem.at[SEM[level] + slot], recv_sem=recv_sem.at[SEM[level] + slot],
            device_id={"seq": s}, device_id_type=MESH,
        ).wait_recv()

    def back_copy(entry):
        level, peer, slot, there = entry
        return pltpu.make_async_remote_copy(
            src_ref=at_slot(outbox[level], level, slot),
            dst_ref=at_slot(rxbox[level], level, there),
            send_sem=back_send.at[SEM[level] + slot],
            recv_sem=back_recv.at[SEM[level] + there],
            device_id={"seq": peer},
            device_id_type=MESH,
        )

    def back_arrival(level, slot):
        here = at_slot(rxbox[level], level, slot)
        pltpu.make_async_remote_copy(
            src_ref=here, dst_ref=here,
            send_sem=back_send.at[SEM[level] + slot], recv_sem=back_recv.at[SEM[level] + slot],
            device_id={"seq": s}, device_id_type=MESH,
        ).wait_recv()

    for entry in peers:
        forward_copy(entry).start()

    tops = []
    for b in range(4):
        rows = pl.ds(BLOCK * b, BLOCK)
        both = dot(perm, jnp.concatenate([q_ref[rows, :], g_ref[rows, :]], axis=1))
        go[rows, :] = both[:, BLOCK:]
        fine = both[:, :BLOCK]
        qs[rows, :] = fine.astype(BF16)
        m1 = halve(fine)
        qs[pl.ds(OFF[1] + 64 * b, 64), :] = m1.astype(BF16)
        m2 = halve(m1)
        qs[pl.ds(OFF[2] + 32 * b, 32), :] = m2.astype(BF16)
        m3 = halve(m2)
        qs[pl.ds(OFF[3] + 16 * b, 16), :] = m3.astype(BF16)
        tops.append(halve(m3))
    qs[pl.ds(OFF[4], 32), :] = jnp.concatenate(tops, axis=0).astype(BF16)

    scale = BLOCK ** (-0.5)
    lane = lax.broadcasted_iota(jnp.int32, (8, 384), 1)

    def off_if(bad):
        return jnp.where(bad, NEG, 0.0).astype(F32)

    no_prev, no_next = off_if(s == 0), off_if(s == seq_count - 1)
    a, y = lax.div(s, 2), lax.div(s, 4)

    def thirds(first, second, last):
        return jnp.where(lane < 128, first, jnp.where(lane < 256, second, last))[:1]

    def slot_bias(i, n):
        even = lax.rem(i, 2) == 0
        return thirds(
            off_if(i < 2), off_if(i + 2 > n - 1),
            off_if((even & (i + 3 > n - 1)) | (jnp.logical_not(even) & (i < 3))),
        )

    bias1 = (
        thirds(no_prev, no_next, no_next),
        thirds(no_prev, no_prev, no_next),
    )
    bias2 = slot_bias(s, seq_count)
    bias3 = slot_bias(a, seq_count // 2)
    bias4 = thirds(jnp.zeros((), F32), off_if((y == 1) | (y == 2)), jnp.zeros((), F32))[:, :256]

    def unit(level, c):
        if level == 0:
            bias = {0: thirds(no_prev, 0.0, 0.0), 3: thirds(0.0, 0.0, no_next)}.get(c)
            return (OFF[0] + BLOCK * c, BLOCK, kv0, BLOCK * c, 384, bias)
        if level == 1:
            return (OFF[1] + BLOCK * c, BLOCK, in1, BLOCK * (1 - c), 384, bias1[c])
        if level == 2:
            return (OFF[2], 128, in2, 0, 384, bias2)
        if level == 3:
            return (OFF[3], 64, in3, 0, 384, bias3)
        return (OFF[4], 32, in4, 0, 256, bias4)

    def forward(level, c=0):
        r0, n, ref, k0, m, bias = unit(level, c)
        rows, keys = pl.ds(r0, n), pl.ds(k0, m)
        sc = dot(qs[rows, :], ref[keys, :BLOCK], NT) * (scale * LOG2E)
        if bias is not None:
            sc = sc + bias
        top = jnp.max(sc, axis=1, keepdims=True)
        e = jnp.exp2(sc - top)
        pk[rows, :] = jnp.broadcast_to(top, (n, BLOCK))
        tot[rows, :] = jnp.broadcast_to(jnp.sum(e, axis=1, keepdims=True), (n, BLOCK))
        eb = e.astype(BF16)
        ee[rows, :m] = eb
        sm[rows, :] = dot(eb, ref[keys, BLOCK:])

    forward(0, 1)
    forward(0, 2)
    for level in (4, 3, 2):
        for slot in range(SLOT_COUNT[level]):
            forward_arrival(level, slot)
        forward(level)
    for slot in range(2):
        forward_arrival(1, slot)
    forward(1, 0)
    forward(1, 1)
    for slot in range(2):
        forward_arrival(0, slot)
    forward(0, 0)
    forward(0, 3)

    for b in range(4):
        where = [pl.ds(OFF[l] + (BLOCK >> l) * b, BLOCK >> l) for l in range(5)]
        peaks = [expand(pk[where[l], :], l) for l in range(5)]
        overall = functools.reduce(jnp.maximum, peaks)
        factors = [jnp.exp2(peaks[l] - overall) * float(1 << l) for l in range(5)]
        den = sum(factors[l] * expand(tot[where[l], :], l) for l in range(5))
        num = sum(factors[l] * expand(sm[where[l], :], l) for l in range(5))
        out = num / den
        att_ref[pl.ds(BLOCK * b, BLOCK), :] = dot(unperm, out.astype(BF16)).astype(BF16)
        cot = go[pl.ds(BLOCK * b, BLOCK), :]
        delta = jnp.broadcast_to(jnp.sum(cot * out, axis=1, keepdims=True), (BLOCK, BLOCK))
        cot, delta = cot / den, delta / den
        for l in range(5):
            gg[where[l], :] = group(factors[l] * cot, l)
            dd[where[l], :] = group(factors[l] * delta, l)

    def backward(level, c=0):
        r0, n, ref, k0, m, _ = unit(level, c)
        rows, keys = pl.ds(r0, n), pl.ds(k0, m)
        gb = gg[rows, :].astype(BF16)
        eb = ee[rows, :m]
        shift = jnp.concatenate([dd[rows, :]] * (m // BLOCK), axis=1)
        ds = eb.astype(F32) * (dot(gb, ref[keys, BLOCK:], NT) - shift)
        ds = (ds * scale).astype(BF16)
        dq[rows, :] = dot(ds, ref[keys, :BLOCK])
        return dot(ds, qs[rows, :], TN), dot(eb, gb, TN)

    def sides(parts):
        return ((parts[0], pl.ds(0, BLOCK)), (parts[1], pl.ds(BLOCK, BLOCK)))

    def start_back(level):
        for entry in peers:
            if entry[0] == level:
                back_copy(entry).start()

    for part, lanes in sides(backward(1, 0)):
        acc1[pl.ds(0, 384), lanes] = part
    for part, lanes in sides(backward(1, 1)):
        bk1[pl.ds(0, 128), lanes] = part[:128].astype(BF16)
        bk1[pl.ds(128, 256), lanes] = (part[128:] + acc1[pl.ds(0, 256), lanes]).astype(BF16)
        bk1[pl.ds(384, 128), lanes] = acc1[pl.ds(256, 128), lanes].astype(BF16)
    start_back(1)
    for level in (2, 3, 4):
        for part, lanes in sides(backward(level)):
            outbox[level][:, lanes] = part.astype(BF16)
        start_back(level)
    for part, lanes in sides(backward(0, 0)):
        bk0[pl.ds(0, 128), lanes] = part[:128].astype(BF16)
        acc0[pl.ds(0, 256), lanes] = part[128:]
    for part, lanes in sides(backward(0, 3)):
        acc0[pl.ds(256, 256), lanes] = part[:256]
        bk0[pl.ds(128, 128), lanes] = part[256:].astype(BF16)
    start_back(0)
    for part, lanes in sides(backward(0, 1)):
        acc0[pl.ds(0, 384), lanes] += part
    for part, lanes in sides(backward(0, 2)):
        acc0[pl.ds(128, 384), lanes] += part

    chunk = 4 * BLOCK // head_count

    def out_copy(index, src, dst, j):
        to = lax.rem(h + j, head_count)
        return pltpu.make_async_remote_copy(
            src_ref=src.at[pl.ds(pl.multiple_of(to * chunk, chunk), chunk), :],
            dst_ref=dst.at[:, pl.ds(pl.multiple_of(h * BLOCK, BLOCK), BLOCK)],
            send_sem=out_send.at[index, to],
            recv_sem=out_recv.at[index, h],
            device_id={"head": to},
            device_id_type=MESH,
        )

    def out_arrival(index, dst, j):
        frm = lax.rem(h + j, head_count)
        here = dst.at[:, pl.ds(pl.multiple_of(frm * BLOCK, BLOCK), BLOCK)]
        pltpu.make_async_remote_copy(
            src_ref=here, dst_ref=here,
            send_sem=out_send.at[index, frm], recv_sem=out_recv.at[index, frm],
            device_id={"head": h}, device_id_type=MESH,
        ).wait_recv()

    def keep(src, dst):
        dst[:, pl.ds(pl.multiple_of(h * BLOCK, BLOCK), BLOCK)] = src[
            pl.ds(pl.multiple_of(h * chunk, chunk), chunk), :
        ]

    for b in range(4):
        total = dq[pl.ds(OFF[4] + 8 * b, 8), :]
        for l in (3, 2, 1, 0):
            total = dq[pl.ds(OFF[l] + (BLOCK >> l) * b, BLOCK >> l), :] + 0.5 * expand(total, 1)
        oq[pl.ds(BLOCK * b, BLOCK), :] = dot(unperm, total.astype(BF16)).astype(BF16)
    for j in range(1, head_count):
        out_copy(0, oq, gq_ref, j).start()
    keep(oq, gq_ref)

    for level in (1, 2, 3, 4, 0):
        for slot in range(SLOT_COUNT[level]):
            back_arrival(level, slot)
    sum4 = sum(rx4[pl.ds(32 * i, 32), :].astype(F32) for i in range(8))
    sum3 = sum(rx3[pl.ds(64 * i, 64), :].astype(F32) for i in range(6)) + 0.5 * expand(sum4, 1)
    sum2 = sum(rx2[pl.ds(128 * i, 128), :].astype(F32) for i in range(3)) + 0.5 * expand(sum3, 1)
    for b in range(4):
        at = 64 * ((b + 2) % 4)
        sum1 = sum(rx1[pl.ds(256 * i + at, 64), :].astype(F32) for i in range(2))
        sum1 = sum1 + 0.5 * expand(sum2[32 * b : 32 * b + 32], 1)
        total = acc0[pl.ds(BLOCK * b, BLOCK), :] + 0.5 * expand(sum1, 1)
        if b == 0:
            total = total + rx0[pl.ds(0, BLOCK), :].astype(F32)
        if b == 3:
            total = total + rx0[pl.ds(BLOCK, BLOCK), :].astype(F32)
        done = dot(unperm, total.astype(BF16)).astype(BF16)
        ok[pl.ds(BLOCK * b, BLOCK), :] = done[:, :BLOCK]
        ov[pl.ds(BLOCK * b, BLOCK), :] = done[:, BLOCK:]
    for j in range(1, head_count):
        out_copy(1, ok, gk_ref, j).start()
        out_copy(2, ov, gv_ref, j).start()
    keep(ok, gk_ref)
    keep(ov, gv_ref)

    for entry in peers:
        forward_copy(entry).wait_send()
        back_copy(entry).wait_send()
    for index, src, dst in ((0, oq, gq_ref), (1, ok, gk_ref), (2, ov, gv_ref)):
        for j in range(1, head_count):
            out_copy(index, src, dst, j).wait_send()
            out_arrival(index, dst, j)


def solution(mesh):
    seq_count, head_count = mesh.shape["seq"], mesh.shape["head"]

    def step(queries, keys, values, grad_out):
        rows, width = queries.shape
        vmem = pl.BlockSpec(memory_space=pltpu.VMEM)
        grad = jax.ShapeDtypeStruct((rows // head_count, width * head_count), BF16)

        def wide(n, dtype=BF16):
            return pltpu.VMEM((n, WIDE), dtype)

        def stacked(dtype, width=BLOCK):
            return pltpu.VMEM((STACK, width), dtype)

        sems = pltpu.SemaphoreType.DMA
        return pl.pallas_call(
            functools.partial(kernel, seq_count, head_count),
            out_shape=(jax.ShapeDtypeStruct((rows, width), BF16), grad, grad, grad),
            in_specs=[vmem] * 4,
            out_specs=(vmem,) * 4,
            scratch_shapes=[
                wide(768), wide(256), wide(128), wide(64), wide(32),
                wide(512), wide(384), wide(384), wide(256),
                stacked(BF16), pltpu.VMEM((rows, width), F32), stacked(BF16, 384),
                stacked(F32), stacked(F32), stacked(F32), stacked(F32), stacked(F32), stacked(F32),
                wide(512, F32), wide(384, F32),
                wide(256), wide(512), wide(384), wide(384), wide(256),
                wide(256), wide(512), wide(384), wide(384), wide(256),
                pltpu.VMEM((rows, width), BF16), pltpu.VMEM((rows, width), BF16),
                pltpu.VMEM((rows, width), BF16),
                sems((SLOTS,)), sems((SLOTS,)), sems((SLOTS,)), sems((SLOTS,)),
                sems((3, head_count)), sems((3, head_count)),
            ],
            compiler_params=pltpu.CompilerParams(
                collective_id=0, has_side_effects=True, vmem_limit_bytes=48 * 1024 * 1024
            ),
        )(queries, keys, values, grad_out)

    return jax.shard_map(
        step,
        mesh=mesh,
        in_specs=(P("seq", "head"),) * 4,
        out_specs=(P("seq", "head"),) + (P(("seq", "head"), None),) * 3,
        check_vma=False,
    )
```

```python
import functools

import jax
import jax.numpy as jnp
from jax import lax
from jax.experimental import pallas as pl
from jax.experimental.pallas import tpu as pltpu
from jax.sharding import PartitionSpec as P

BLOCK = 128
WIDE = 256
NEG = -1e30
F32 = jnp.float32
BF16 = jnp.bfloat16
LOG2E = 1.4426950408889634
MESH = pl.DeviceIdType.MESH
OFF = (0, 512, 768, 896, 960)
STACK = 992
SEM = (0, 2, 4, 7, 13)
SLOTS = 21
ROWS = (128, 192, 128, 64, 32)

NN = (((1,), (0,)), ((), ()))
NT = (((1,), (1,)), ((), ()))
TN = (((0,), (0,)), ((), ()))


def dot(a, b, dims=NN):
    return lax.dot_general(a, b, dims, preferred_element_type=F32)


def halve(x):
    n, w = x.shape
    x = x.reshape(n // 16, 2, 8, w)
    m = (x[:, 0] + x[:, 1]) * 0.5
    return m.astype(BF16).astype(F32).reshape(n // 2, w)


def expand(x, level):
    n, w = x.shape
    if level == 0:
        return x
    x = x.reshape(n // 8, 1, 8, w)
    x = jnp.broadcast_to(x, (n // 8, 1 << level, 8, w))
    return x.reshape(n << level, w)


def group(x, level):
    n, w = x.shape
    if level == 0:
        return x
    return x.reshape(n >> (level + 3), 1 << level, 8, w).sum(axis=1).reshape(n >> level, w)


def peers_of(s, seq_count):
    out = []
    prev, after = lax.rem(s + seq_count - 1, seq_count), lax.rem(s + 1, seq_count)
    a, e = lax.div(s, 2), lax.rem(s, 2)
    y, x = lax.div(s, 4), lax.rem(s, 4)

    def third(i, n):
        turn = 3 - 6 * lax.rem(i, 2)
        return lax.rem(i + n + turn, n), (i + turn >= 0) & (i + turn < n)

    blocks = seq_count // 2
    for f in range(4):
        out.append((4, lax.rem(y + 2, 4) * 4 + f, f, x, None))
    for f in range(4):
        out.append((4, (3 - y) * 4 + f, 4 + f, 4 + x, (y == 0) | (y == 3)))
    far3, far3_ok = third(a, blocks)
    for f in range(2):
        out.append((3, far3 * 2 + f, 4 + f, 4 + e, far3_ok))
    for f in range(2):
        out.append((3, lax.rem(a + blocks - 2, blocks) * 2 + f, f, 2 + e, a >= 2))
        out.append((3, lax.rem(a + 2, blocks) * 2 + f, 2 + f, e, a + 2 < blocks))
    far2, far2_ok = third(s, seq_count)
    out.append((2, far2, 2, 2, far2_ok))
    out.append((2, lax.rem(s + seq_count - 2, seq_count), 0, 1, s >= 2))
    out.append((2, lax.rem(s + 2, seq_count), 1, 0, s + 2 < seq_count))
    out.append((1, prev, 0, 1, s > 0))
    out.append((1, after, 1, 0, s + 1 < seq_count))
    out.append((0, prev, 0, 1, s > 0))
    out.append((0, after, 1, 0, s + 1 < seq_count))
    return out


def when(ok, act):
    if ok is None:
        act()
    else:
        pl.when(ok)(act)


def kernel(
    seq_count, head_count,
    q_hbm, k_hbm, v_hbm, g_hbm,
    att_ref, gq_ref, gk_ref, gv_ref,
    kv0, kv1, kv2, kv3, kv4, in1, in2, in3, in4,
    qs, go, ee, pk, tot, sm, gg, dd, dq,
    acc0, acc1, edge, bk0, bk1, bk2, bk3, bk4, rx0, rx1, rx2, rx3, rx4,
    oq, ok, ov, q_ref, k_ref, v_ref, g_ref, load_sem,
    send_sem, recv_sem, back_send, back_recv, out_send, out_recv,
):
    s, h = lax.axis_index("seq"), lax.axis_index("head")
    barrier = pltpu.get_barrier_semaphore()
    loads = [
        pltpu.make_async_copy(src, dst, load_sem.at[i])
        for i, (src, dst) in enumerate(
            ((k_hbm, k_ref), (v_hbm, v_ref), (q_hbm, q_ref), (g_hbm, g_ref))
        )
    ]
    for load in loads:
        load.start()
    for j in range(1, seq_count):
        pl.semaphore_signal(
            barrier, inc=1, device_id={"seq": lax.rem(s + j, seq_count)}, device_id_type=MESH
        )
    for j in range(1, head_count):
        pl.semaphore_signal(
            barrier, inc=1, device_id={"head": lax.rem(h + j, head_count)}, device_id_type=MESH
        )

    row = lax.broadcasted_iota(jnp.int32, (BLOCK, BLOCK), 0)
    col = lax.broadcasted_iota(jnp.int32, (BLOCK, BLOCK), 1)
    perm = jnp.where(col == (row & 7) * 16 + (row >> 3), 1.0, 0.0).astype(BF16)
    unperm = jnp.where(col == (row & 15) * 8 + (row >> 4), 1.0, 0.0).astype(BF16)

    loads[0].wait()
    loads[1].wait()
    own = (kv0, kv1, kv2, kv3, kv4)
    tops = []
    for b in range(4):
        rows = pl.ds(BLOCK * b, BLOCK)
        fine = dot(perm, jnp.concatenate([k_ref[rows, :], v_ref[rows, :]], axis=1))
        kv0[pl.ds(BLOCK + BLOCK * b, BLOCK), :] = fine.astype(BF16)
        m1 = halve(fine)
        kv1[pl.ds(64 * (3 - b), 64), :] = m1.astype(BF16)
        m2 = halve(m1)
        kv2[pl.ds(32 * b, 32), :] = m2.astype(BF16)
        m3 = halve(m2)
        kv3[pl.ds(16 * b, 16), :] = m3.astype(BF16)
        tops.append(halve(m3))
    kv4[...] = jnp.concatenate(tops, axis=0).astype(BF16)

    pl.semaphore_wait(barrier, seq_count - 1 + head_count - 1)

    peers = peers_of(s, seq_count)
    inbox = (kv0, in1, in2, in3, in4)
    outbox = (bk0, bk1, bk2, bk3, bk4)
    rxbox = (rx0, rx1, rx2, rx3, rx4)

    def at_slot(ref, level, slot):
        n = ROWS[level]
        return ref.at[pl.ds(n * slot, n), :]

    def in_slot(level, slot):
        if level == 0:
            return kv0.at[pl.ds(640 * slot, BLOCK), :]
        if level == 1:
            return in1.at[pl.ds(64 + 192 * slot, 192), :]
        return at_slot(inbox[level], level, slot)

    def out_slot(level, slot):
        if level == 0:
            return kv0.at[pl.ds(BLOCK + 384 * slot, BLOCK), :]
        if level == 1:
            return kv1.at[pl.ds(64 * slot, 192), :]
        return own[level]

    def forward_copy(entry):
        level, peer, slot, there, _ = entry
        return pltpu.make_async_remote_copy(
            src_ref=out_slot(level, slot),
            dst_ref=in_slot(level, there),
            send_sem=send_sem.at[SEM[level] + slot],
            recv_sem=recv_sem.at[SEM[level] + there],
            device_id={"seq": peer},
            device_id_type=MESH,
        )

    def forward_arrival(entry):
        level, peer, slot = entry[:3]
        here = in_slot(level, slot)
        pltpu.make_async_remote_copy(
            src_ref=here, dst_ref=here,
            send_sem=send_sem.at[SEM[level] + slot], recv_sem=recv_sem.at[SEM[level] + slot],
            device_id={"seq": peer}, device_id_type=MESH,
        ).wait_recv()

    def back_slot(level, slot):
        if level == 1:
            return bk1.at[pl.ds(64 + 192 * slot, 192), :]
        return at_slot(outbox[level], level, slot)

    def back_copy(entry):
        level, peer, slot, there, _ = entry
        return pltpu.make_async_remote_copy(
            src_ref=back_slot(level, slot),
            dst_ref=at_slot(rxbox[level], level, there),
            send_sem=back_send.at[SEM[level] + slot],
            recv_sem=back_recv.at[SEM[level] + there],
            device_id={"seq": peer},
            device_id_type=MESH,
        )

    def back_arrival(entry):
        level, peer, slot = entry[:3]
        here = at_slot(rxbox[level], level, slot)
        pltpu.make_async_remote_copy(
            src_ref=here, dst_ref=here,
            send_sem=back_send.at[SEM[level] + slot], recv_sem=back_recv.at[SEM[level] + slot],
            device_id={"seq": peer}, device_id_type=MESH,
        ).wait_recv()

    def at_level(level):
        return [entry for entry in peers if entry[0] == level]

    for entry in peers:
        when(entry[4], lambda: forward_copy(entry).start())

    def clear(entry):
        level, slot = entry[0], entry[2]
        for ref in (in_slot(level, slot), at_slot(rxbox[level], level, slot)):
            ref[...] = jnp.zeros(ref.shape, BF16)

    for entry in peers:
        if entry[4] is not None:
            when(jnp.logical_not(entry[4]), lambda: clear(entry))

    loads[2].wait()
    loads[3].wait()
    tops = []
    for b in range(4):
        rows = pl.ds(BLOCK * b, BLOCK)
        both = dot(perm, jnp.concatenate([q_ref[rows, :], g_ref[rows, :]], axis=1))
        go[rows, :] = both[:, BLOCK:]
        fine = both[:, :BLOCK]
        qs[rows, :] = fine.astype(BF16)
        m1 = halve(fine)
        qs[pl.ds(OFF[1] + 64 * b, 64), :] = m1.astype(BF16)
        m2 = halve(m1)
        qs[pl.ds(OFF[2] + 32 * b, 32), :] = m2.astype(BF16)
        m3 = halve(m2)
        qs[pl.ds(OFF[3] + 16 * b, 16), :] = m3.astype(BF16)
        tops.append(halve(m3))
    qs[pl.ds(OFF[4], 32), :] = jnp.concatenate(tops, axis=0).astype(BF16)

    scale = BLOCK ** (-0.5)
    lane = lax.broadcasted_iota(jnp.int32, (8, 384), 1)

    def off_if(bad):
        return jnp.where(bad, NEG, 0.0).astype(F32)

    no_prev, no_next = off_if(s == 0), off_if(s == seq_count - 1)
    a, y = lax.div(s, 2), lax.div(s, 4)

    def thirds(first, second, last):
        return jnp.where(lane < 128, first, jnp.where(lane < 256, second, last))[:1]

    def slot_bias(i, n):
        even = lax.rem(i, 2) == 0
        return thirds(
            off_if(i < 2), off_if(i + 2 > n - 1),
            off_if((even & (i + 3 > n - 1)) | (jnp.logical_not(even) & (i < 3))),
        )

    bias1 = (
        thirds(no_prev, no_next, no_next),
        thirds(no_prev, no_prev, no_next),
    )
    bias2 = slot_bias(s, seq_count)
    bias3 = slot_bias(a, seq_count // 2)
    bias4 = thirds(jnp.zeros((), F32), off_if((y == 1) | (y == 2)), jnp.zeros((), F32))[:, :256]

    def unit(level, c):
        if level == 0:
            bias = {0: thirds(no_prev, 0.0, 0.0), 3: thirds(0.0, 0.0, no_next)}.get(c)
            return (OFF[0] + BLOCK * c, BLOCK, kv0, BLOCK * c, 384, bias)
        if level == 1:
            return (OFF[1] + BLOCK * c, BLOCK, in1, BLOCK * (1 - c), 384, bias1[c])
        if level == 2:
            return (OFF[2], 128, in2, 0, 384, bias2)
        if level == 3:
            return (OFF[3], 64, in3, 0, 384, bias3)
        return (OFF[4], 32, in4, 0, 256, bias4)

    def forward(level, c=0):
        r0, n, ref, k0, m, bias = unit(level, c)
        rows, keys = pl.ds(r0, n), pl.ds(k0, m)
        sc = dot(qs[rows, :], ref[keys, :BLOCK], NT) * (scale * LOG2E)
        if bias is not None:
            sc = sc + bias
        top = jnp.max(sc, axis=1, keepdims=True)
        e = jnp.exp2(sc - top)
        pk[rows, :] = jnp.broadcast_to(top, (n, BLOCK))
        tot[rows, :] = jnp.broadcast_to(jnp.sum(e, axis=1, keepdims=True), (n, BLOCK))
        eb = e.astype(BF16)
        ee[rows, :m] = eb
        sm[rows, :] = dot(eb, ref[keys, BLOCK:])

    forward(0, 1)
    forward(0, 2)
    for entry in at_level(0):
        when(entry[4], lambda: forward_arrival(entry))
    in1[pl.ds(0, 64), :] = halve(kv0[pl.ds(0, BLOCK), :].astype(F32)).astype(BF16)
    in1[pl.ds(448, 64), :] = halve(kv0[pl.ds(640, BLOCK), :].astype(F32)).astype(BF16)
    forward(0, 0)
    forward(0, 3)
    for level in (3, 4, 2):
        for entry in at_level(level):
            when(entry[4], lambda: forward_arrival(entry))
        forward(level)
    for entry in at_level(1):
        when(entry[4], lambda: forward_arrival(entry))
    forward(1, 0)
    forward(1, 1)

    for b in range(4):
        where = [pl.ds(OFF[l] + (BLOCK >> l) * b, BLOCK >> l) for l in range(5)]
        peaks = [expand(pk[where[l], :], l) for l in range(5)]
        overall = functools.reduce(jnp.maximum, peaks)
        factors = [jnp.exp2(peaks[l] - overall) * float(1 << l) for l in range(5)]
        den = sum(factors[l] * expand(tot[where[l], :], l) for l in range(5))
        num = sum(factors[l] * expand(sm[where[l], :], l) for l in range(5))
        out = num / den
        att_ref[pl.ds(BLOCK * b, BLOCK), :] = dot(unperm, out.astype(BF16)).astype(BF16)
        cot = go[pl.ds(BLOCK * b, BLOCK), :]
        delta = jnp.broadcast_to(jnp.sum(cot * out, axis=1, keepdims=True), (BLOCK, BLOCK))
        cot, delta = cot / den, delta / den
        for l in range(5):
            gg[where[l], :] = group(factors[l] * cot, l)
            dd[where[l], :] = group(factors[l] * delta, l)

    def backward(level, c=0):
        r0, n, ref, k0, m, _ = unit(level, c)
        rows, keys = pl.ds(r0, n), pl.ds(k0, m)
        gb = gg[rows, :].astype(BF16)
        eb = ee[rows, :m]
        shift = jnp.concatenate([dd[rows, :]] * (m // BLOCK), axis=1)
        ds = eb.astype(F32) * (dot(gb, ref[keys, BLOCK:], NT) - shift)
        ds = (ds * scale).astype(BF16)
        dq[rows, :] = dot(ds, ref[keys, :BLOCK])
        return dot(ds, qs[rows, :], TN), dot(eb, gb, TN)

    def sides(parts):
        return ((parts[0], pl.ds(0, BLOCK)), (parts[1], pl.ds(BLOCK, BLOCK)))

    def start_back(level):
        for entry in peers:
            if entry[0] == level:
                when(entry[4], lambda: back_copy(entry).start())

    for part, lanes in sides(backward(1, 0)):
        acc1[pl.ds(0, 384), lanes] = part
    for part, lanes in sides(backward(1, 1)):
        edge[pl.ds(0, 64), lanes] = part[:64]
        bk1[pl.ds(64, 64), lanes] = part[64:128].astype(BF16)
        bk1[pl.ds(128, 256), lanes] = (part[128:] + acc1[pl.ds(0, 256), lanes]).astype(BF16)
        bk1[pl.ds(384, 64), lanes] = acc1[pl.ds(256, 64), lanes].astype(BF16)
        edge[pl.ds(64, 64), lanes] = acc1[pl.ds(320, 64), lanes]
    start_back(1)
    for level in (2, 3, 4):
        for part, lanes in sides(backward(level)):
            outbox[level][:, lanes] = part.astype(BF16)
        start_back(level)
    for part, lanes in sides(backward(0, 0)):
        fold = 0.5 * expand(edge[pl.ds(0, 64), lanes], 1)
        bk0[pl.ds(0, 128), lanes] = (part[:128] + fold).astype(BF16)
        acc0[pl.ds(0, 256), lanes] = part[128:]
    for part, lanes in sides(backward(0, 3)):
        acc0[pl.ds(256, 256), lanes] = part[:256]
        fold = 0.5 * expand(edge[pl.ds(64, 64), lanes], 1)
        bk0[pl.ds(128, 128), lanes] = (part[256:] + fold).astype(BF16)
    start_back(0)
    for part, lanes in sides(backward(0, 1)):
        acc0[pl.ds(0, 384), lanes] += part
    for part, lanes in sides(backward(0, 2)):
        acc0[pl.ds(128, 384), lanes] += part

    chunk = 4 * BLOCK // head_count

    def out_copy(index, src, dst, j):
        to = lax.rem(h + j, head_count)
        return pltpu.make_async_remote_copy(
            src_ref=src.at[pl.ds(pl.multiple_of(to * chunk, chunk), chunk), :],
            dst_ref=dst.at[:, pl.ds(pl.multiple_of(h * BLOCK, BLOCK), BLOCK)],
            send_sem=out_send.at[index, to],
            recv_sem=out_recv.at[index, h],
            device_id={"head": to},
            device_id_type=MESH,
        )

    def out_arrival(index, dst, j):
        frm = lax.rem(h + j, head_count)
        here = dst.at[:, pl.ds(pl.multiple_of(frm * BLOCK, BLOCK), BLOCK)]
        pltpu.make_async_remote_copy(
            src_ref=here, dst_ref=here,
            send_sem=out_send.at[index, frm], recv_sem=out_recv.at[index, frm],
            device_id={"head": h}, device_id_type=MESH,
        ).wait_recv()

    def keep(src, dst):
        dst[:, pl.ds(pl.multiple_of(h * BLOCK, BLOCK), BLOCK)] = src[
            pl.ds(pl.multiple_of(h * chunk, chunk), chunk), :
        ]

    for b in range(4):
        total = dq[pl.ds(OFF[4] + 8 * b, 8), :]
        for l in (3, 2, 1, 0):
            total = dq[pl.ds(OFF[l] + (BLOCK >> l) * b, BLOCK >> l), :] + 0.5 * expand(total, 1)
        oq[pl.ds(BLOCK * b, BLOCK), :] = dot(unperm, total.astype(BF16)).astype(BF16)
    for j in range(1, head_count):
        out_copy(0, oq, gq_ref, j).start()
    keep(oq, gq_ref)

    for level in (1, 2, 3, 4, 0):
        for entry in at_level(level):
            when(entry[4], lambda: back_arrival(entry))
    sum4 = sum(rx4[pl.ds(32 * i, 32), :].astype(F32) for i in range(8))
    sum3 = sum(rx3[pl.ds(64 * i, 64), :].astype(F32) for i in range(6)) + 0.5 * expand(sum4, 1)
    sum2 = sum(rx2[pl.ds(128 * i, 128), :].astype(F32) for i in range(3)) + 0.5 * expand(sum3, 1)
    for b in range(4):
        sum1 = jnp.zeros((64, WIDE), F32)
        if b > 0:
            sum1 = sum1 + rx1[pl.ds(64 * (3 - b), 64), :].astype(F32)
        if b < 3:
            sum1 = sum1 + rx1[pl.ds(192 + 64 * (2 - b), 64), :].astype(F32)
        sum1 = sum1 + 0.5 * expand(sum2[32 * b : 32 * b + 32], 1)
        total = acc0[pl.ds(BLOCK * b, BLOCK), :] + 0.5 * expand(sum1, 1)
        if b == 0:
            total = total + rx0[pl.ds(0, BLOCK), :].astype(F32)
        if b == 3:
            total = total + rx0[pl.ds(BLOCK, BLOCK), :].astype(F32)
        done = dot(unperm, total.astype(BF16)).astype(BF16)
        ok[pl.ds(BLOCK * b, BLOCK), :] = done[:, :BLOCK]
        ov[pl.ds(BLOCK * b, BLOCK), :] = done[:, BLOCK:]
    for j in range(1, head_count):
        out_copy(1, ok, gk_ref, j).start()
        out_copy(2, ov, gv_ref, j).start()
    keep(ok, gk_ref)
    keep(ov, gv_ref)

    for entry in peers:
        when(entry[4], lambda: (forward_copy(entry).wait_send(), back_copy(entry).wait_send()) and None)
    for index, src, dst in ((0, oq, gq_ref), (1, ok, gk_ref), (2, ov, gv_ref)):
        for j in range(1, head_count):
            out_copy(index, src, dst, j).wait_send()
            out_arrival(index, dst, j)


def write_out(a, b, c, d, a_out, b_out, c_out, d_out, sem):
    copies = [
        pltpu.make_async_copy(src, dst, sem.at[i])
        for i, (src, dst) in enumerate(((a, a_out), (b, b_out), (c, c_out), (d, d_out)))
    ]
    for copy in copies:
        copy.start()
    for copy in copies:
        copy.wait()


def solution(mesh):
    seq_count, head_count = mesh.shape["seq"], mesh.shape["head"]

    def step(queries, keys, values, grad_out):
        rows, width = queries.shape
        vmem = pl.BlockSpec(memory_space=pltpu.VMEM)
        grad = jax.ShapeDtypeStruct((rows // head_count, width * head_count), BF16)

        def wide(n, dtype=BF16):
            return pltpu.VMEM((n, WIDE), dtype)

        def stacked(dtype, width=BLOCK):
            return pltpu.VMEM((STACK, width), dtype)

        sems = pltpu.SemaphoreType.DMA
        results = pl.pallas_call(
            functools.partial(kernel, seq_count, head_count),
            out_shape=(jax.ShapeDtypeStruct((rows, width), BF16), grad, grad, grad),
            in_specs=[pl.BlockSpec(memory_space=pltpu.HBM)] * 4,
            out_specs=(vmem,) * 4,
            scratch_shapes=[
                wide(768), wide(256), wide(128), wide(64), wide(32),
                wide(512), wide(384), wide(384), wide(256),
                stacked(BF16), pltpu.VMEM((rows, width), F32), stacked(BF16, 384),
                stacked(F32), stacked(F32), stacked(F32), stacked(F32), stacked(F32), stacked(F32),
                wide(512, F32), wide(384, F32), wide(128, F32),
                wide(256), wide(512), wide(384), wide(384), wide(256),
                wide(256), wide(384), wide(384), wide(384), wide(256),
                *[pltpu.VMEM((rows, width), BF16) for _ in range(7)],
                sems((4,)),
                sems((SLOTS,)), sems((SLOTS,)), sems((SLOTS,)), sems((SLOTS,)),
                sems((3, head_count)), sems((3, head_count)),
            ],
            compiler_params=pltpu.CompilerParams(
                collective_id=0, has_side_effects=True, vmem_limit_bytes=56000000
            ),
        )(queries, keys, values, grad_out)
        return pl.pallas_call(
            write_out,
            out_shape=tuple(jax.ShapeDtypeStruct(r.shape, r.dtype) for r in results),
            in_specs=[vmem] * 4,
            out_specs=(pl.BlockSpec(memory_space=pltpu.HBM),) * 4,
            scratch_shapes=[sems((4,))],
            compiler_params=pltpu.CompilerParams(vmem_limit_bytes=1024 * 1024),
        )(*results)

    return jax.shard_map(
        step,
        mesh=mesh,
        in_specs=(P("seq", "head"),) * 4,
        out_specs=(P("seq", "head"),) + (P(("seq", "head"), None),) * 3,
        check_vma=False,
    )
```

```python
import functools

import jax
import jax.numpy as jnp
from jax import lax
from jax.experimental import pallas as pl
from jax.experimental.pallas import tpu as pltpu
from jax.sharding import PartitionSpec as P

BLOCK = 128
WIDE = 256
NEG = -1e30
F32 = jnp.float32
BF16 = jnp.bfloat16
LOG2E = 1.4426950408889634
MESH = pl.DeviceIdType.MESH
OFF = (0, 512, 768, 896, 960)
STACK = 992
SEM = (0, 2, 4, 7, 13)
SLOTS = 21
ROWS = (128, 192, 128, 64, 32)

SEND_ORDER = (0, 1, 4, 3, 2)
BACK_ORDER = (2, 3, 4)
NN = (((1,), (0,)), ((), ()))
NT = (((1,), (1,)), ((), ()))
TN = (((0,), (0,)), ((), ()))


def dot(a, b, dims=NN):
    return lax.dot_general(a, b, dims, preferred_element_type=F32)


def halve(x):
    n, w = x.shape
    x = x.reshape(n // 16, 2, 8, w)
    m = (x[:, 0] + x[:, 1]) * 0.5
    return m.astype(BF16).astype(F32).reshape(n // 2, w)


def expand(x, level):
    n, w = x.shape
    if level == 0:
        return x
    x = x.reshape(n // 8, 1, 8, w)
    x = jnp.broadcast_to(x, (n // 8, 1 << level, 8, w))
    return x.reshape(n << level, w)


def group(x, level):
    n, w = x.shape
    if level == 0:
        return x
    return x.reshape(n >> (level + 3), 1 << level, 8, w).sum(axis=1).reshape(n >> level, w)


def peers_of(s, seq_count):
    out = []
    prev, after = lax.rem(s + seq_count - 1, seq_count), lax.rem(s + 1, seq_count)
    a, e = lax.div(s, 2), lax.rem(s, 2)
    y, x = lax.div(s, 4), lax.rem(s, 4)

    def third(i, n):
        turn = 3 - 6 * lax.rem(i, 2)
        return lax.rem(i + n + turn, n), (i + turn >= 0) & (i + turn < n)

    blocks = seq_count // 2
    for f in range(4):
        out.append((4, lax.rem(y + 2, 4) * 4 + f, f, x, None))
    for f in range(4):
        out.append((4, (3 - y) * 4 + f, 4 + f, 4 + x, (y == 0) | (y == 3)))
    far3, far3_ok = third(a, blocks)
    for f in range(2):
        out.append((3, far3 * 2 + f, 4 + f, 4 + e, far3_ok))
    for f in range(2):
        out.append((3, lax.rem(a + blocks - 2, blocks) * 2 + f, f, 2 + e, a >= 2))
        out.append((3, lax.rem(a + 2, blocks) * 2 + f, 2 + f, e, a + 2 < blocks))
    far2, far2_ok = third(s, seq_count)
    out.append((2, far2, 2, 2, far2_ok))
    out.append((2, lax.rem(s + seq_count - 2, seq_count), 0, 1, s >= 2))
    out.append((2, lax.rem(s + 2, seq_count), 1, 0, s + 2 < seq_count))
    out.append((1, prev, 0, 1, s > 0))
    out.append((1, after, 1, 0, s + 1 < seq_count))
    out.append((0, prev, 0, 1, s > 0))
    out.append((0, after, 1, 0, s + 1 < seq_count))
    return out


def when(ok, act):
    if ok is None:
        act()
    else:
        pl.when(ok)(act)


def kernel(
    seq_count, head_count,
    q_hbm, k_hbm, v_hbm, g_hbm,
    att_ref, gq_ref, gk_ref, gv_ref,
    kv0, kv1, kv2, kv3, kv4, in1, in2, in3, in4,
    qs, go, ee, pk, tot, sm, gg, dd, dq,
    acc0, acc1, edge, bk0, bk1, bk2, bk3, bk4, rx0, rx1, rx2, rx3, rx4,
    oq, ok, ov, oc, coarse, q_ref, k_ref, v_ref, g_ref, load_sem,
    send_sem, recv_sem, back_send, back_recv, out_send, out_recv,
):
    s, h = lax.axis_index("seq"), lax.axis_index("head")
    barrier = pltpu.get_barrier_semaphore()
    loads = [
        pltpu.make_async_copy(src, dst, load_sem.at[i])
        for i, (src, dst) in enumerate(
            ((k_hbm, k_ref), (v_hbm, v_ref), (q_hbm, q_ref), (g_hbm, g_ref))
        )
    ]
    for load in loads:
        load.start()
    for j in range(1, seq_count):
        pl.semaphore_signal(
            barrier, inc=1, device_id={"seq": lax.rem(s + j, seq_count)}, device_id_type=MESH
        )
    for j in range(1, head_count):
        pl.semaphore_signal(
            barrier, inc=1, device_id={"head": lax.rem(h + j, head_count)}, device_id_type=MESH
        )

    row = lax.broadcasted_iota(jnp.int32, (BLOCK, BLOCK), 0)
    col = lax.broadcasted_iota(jnp.int32, (BLOCK, BLOCK), 1)
    perm = jnp.where(col == (row & 7) * 16 + (row >> 3), 1.0, 0.0).astype(BF16)
    unperm = jnp.where(col == (row & 15) * 8 + (row >> 4), 1.0, 0.0).astype(BF16)

    loads[0].wait()
    loads[1].wait()
    own = (kv0, kv1, kv2, kv3, kv4)
    tops = []
    for b in range(4):
        rows = pl.ds(BLOCK * b, BLOCK)
        fine = dot(perm, jnp.concatenate([k_ref[rows, :], v_ref[rows, :]], axis=1))
        kv0[pl.ds(BLOCK + BLOCK * b, BLOCK), :] = fine.astype(BF16)
        m1 = halve(fine)
        kv1[pl.ds(64 * (3 - b), 64), :] = m1.astype(BF16)
        m2 = halve(m1)
        kv2[pl.ds(32 * b, 32), :] = m2.astype(BF16)
        m3 = halve(m2)
        kv3[pl.ds(16 * b, 16), :] = m3.astype(BF16)
        tops.append(halve(m3))
    kv4[...] = jnp.concatenate(tops, axis=0).astype(BF16)

    pl.semaphore_wait(barrier, seq_count - 1 + head_count - 1)

    peers = peers_of(s, seq_count)
    inbox = (kv0, in1, in2, in3, in4)
    outbox = (bk0, bk1, bk2, bk3, bk4)
    rxbox = (rx0, rx1, rx2, rx3, rx4)

    def at_slot(ref, level, slot):
        n = ROWS[level]
        return ref.at[pl.ds(n * slot, n), :]

    def in_slot(level, slot):
        if level == 0:
            return kv0.at[pl.ds(640 * slot, BLOCK), :]
        if level == 1:
            return in1.at[pl.ds(64 + 192 * slot, 192), :]
        return at_slot(inbox[level], level, slot)

    def out_slot(level, slot):
        if level == 0:
            return kv0.at[pl.ds(BLOCK + 384 * slot, BLOCK), :]
        if level == 1:
            return kv1.at[pl.ds(64 * slot, 192), :]
        return own[level]

    def forward_copy(entry):
        level, peer, slot, there, _ = entry
        return pltpu.make_async_remote_copy(
            src_ref=out_slot(level, slot),
            dst_ref=in_slot(level, there),
            send_sem=send_sem.at[SEM[level] + slot],
            recv_sem=recv_sem.at[SEM[level] + there],
            device_id={"seq": peer},
            device_id_type=MESH,
        )

    def forward_arrival(entry):
        level, peer, slot = entry[:3]
        here = in_slot(level, slot)
        pltpu.make_async_remote_copy(
            src_ref=here, dst_ref=here,
            send_sem=send_sem.at[SEM[level] + slot], recv_sem=recv_sem.at[SEM[level] + slot],
            device_id={"seq": peer}, device_id_type=MESH,
        ).wait_recv()

    def back_slot(level, slot):
        if level == 1:
            return bk1.at[pl.ds(64 + 192 * slot, 192), :]
        return at_slot(outbox[level], level, slot)

    def back_copy(entry):
        level, peer, slot, there, _ = entry
        return pltpu.make_async_remote_copy(
            src_ref=back_slot(level, slot),
            dst_ref=at_slot(rxbox[level], level, there),
            send_sem=back_send.at[SEM[level] + slot],
            recv_sem=back_recv.at[SEM[level] + there],
            device_id={"seq": peer},
            device_id_type=MESH,
        )

    def back_arrival(entry):
        level, peer, slot = entry[:3]
        here = at_slot(rxbox[level], level, slot)
        pltpu.make_async_remote_copy(
            src_ref=here, dst_ref=here,
            send_sem=back_send.at[SEM[level] + slot], recv_sem=back_recv.at[SEM[level] + slot],
            device_id={"seq": peer}, device_id_type=MESH,
        ).wait_recv()

    def at_level(level):
        return [entry for entry in peers if entry[0] == level]

    for level in SEND_ORDER:
        for entry in at_level(level):
            when(entry[4], lambda: forward_copy(entry).start())

    def clear(entry):
        level, slot = entry[0], entry[2]
        for ref in (in_slot(level, slot), at_slot(rxbox[level], level, slot)):
            ref[...] = jnp.zeros(ref.shape, BF16)

    for entry in peers:
        if entry[4] is not None:
            when(jnp.logical_not(entry[4]), lambda: clear(entry))

    loads[2].wait()
    loads[3].wait()
    tops = []
    for b in range(4):
        rows = pl.ds(BLOCK * b, BLOCK)
        both = dot(perm, jnp.concatenate([q_ref[rows, :], g_ref[rows, :]], axis=1))
        go[rows, :] = both[:, BLOCK:]
        fine = both[:, :BLOCK]
        qs[rows, :] = fine.astype(BF16)
        m1 = halve(fine)
        qs[pl.ds(OFF[1] + 64 * b, 64), :] = m1.astype(BF16)
        m2 = halve(m1)
        qs[pl.ds(OFF[2] + 32 * b, 32), :] = m2.astype(BF16)
        m3 = halve(m2)
        qs[pl.ds(OFF[3] + 16 * b, 16), :] = m3.astype(BF16)
        tops.append(halve(m3))
    qs[pl.ds(OFF[4], 32), :] = jnp.concatenate(tops, axis=0).astype(BF16)

    scale = BLOCK ** (-0.5)
    lane = lax.broadcasted_iota(jnp.int32, (8, 384), 1)

    def off_if(bad):
        return jnp.where(bad, NEG, 0.0).astype(F32)

    no_prev, no_next = off_if(s == 0), off_if(s == seq_count - 1)
    a, y = lax.div(s, 2), lax.div(s, 4)

    def thirds(first, second, last):
        return jnp.where(lane < 128, first, jnp.where(lane < 256, second, last))[:1]

    def slot_bias(i, n):
        even = lax.rem(i, 2) == 0
        return thirds(
            off_if(i < 2), off_if(i + 2 > n - 1),
            off_if((even & (i + 3 > n - 1)) | (jnp.logical_not(even) & (i < 3))),
        )

    bias1 = (
        thirds(no_prev, no_next, no_next),
        thirds(no_prev, no_prev, no_next),
    )
    bias2 = slot_bias(s, seq_count)
    bias3 = slot_bias(a, seq_count // 2)
    bias4 = thirds(jnp.zeros((), F32), off_if((y == 1) | (y == 2)), jnp.zeros((), F32))[:, :256]

    def unit(level, c):
        if level == 0:
            bias = {0: thirds(no_prev, 0.0, 0.0), 3: thirds(0.0, 0.0, no_next)}.get(c)
            return (OFF[0] + BLOCK * c, BLOCK, kv0, BLOCK * c, 384, bias)
        if level == 1:
            return (OFF[1] + BLOCK * c, BLOCK, in1, BLOCK * (1 - c), 384, bias1[c])
        if level == 2:
            return (OFF[2], 128, in2, 0, 384, bias2)
        if level == 3:
            return (OFF[3], 64, in3, 0, 384, bias3)
        return (OFF[4], 32, in4, 0, 256, bias4)

    def forward(level, c=0):
        r0, n, ref, k0, m, bias = unit(level, c)
        rows, keys = pl.ds(r0, n), pl.ds(k0, m)
        sc = dot(qs[rows, :], ref[keys, :BLOCK], NT) * (scale * LOG2E)
        if bias is not None:
            sc = sc + bias
        top = jnp.max(sc, axis=1, keepdims=True)
        e = jnp.exp2(sc - top)
        pk[rows, :] = jnp.broadcast_to(top, (n, BLOCK))
        tot[rows, :] = jnp.broadcast_to(jnp.sum(e, axis=1, keepdims=True), (n, BLOCK))
        eb = e.astype(BF16)
        ee[rows, :m] = eb
        sm[rows, :] = dot(eb, ref[keys, BLOCK:])

    forward(0, 1)
    forward(0, 2)
    for level in SEND_ORDER:
        for entry in at_level(level):
            when(entry[4], lambda: forward_arrival(entry))
        if level == 0:
            in1[pl.ds(0, 64), :] = halve(kv0[pl.ds(0, BLOCK), :].astype(F32)).astype(BF16)
            in1[pl.ds(448, 64), :] = halve(kv0[pl.ds(640, BLOCK), :].astype(F32)).astype(BF16)
            forward(0, 0)
            forward(0, 3)
        elif level == 1:
            forward(1, 0)
            forward(1, 1)
        else:
            forward(level)

    for b in range(4):
        where = [pl.ds(OFF[l] + (BLOCK >> l) * b, BLOCK >> l) for l in range(5)]
        peaks = [expand(pk[where[l], :], l) for l in range(5)]
        overall = functools.reduce(jnp.maximum, peaks)
        factors = [jnp.exp2(peaks[l] - overall) * float(1 << l) for l in range(5)]
        den = sum(factors[l] * expand(tot[where[l], :], l) for l in range(5))
        num = sum(factors[l] * expand(sm[where[l], :], l) for l in range(5))
        inverse = 1.0 / den
        out = num * inverse
        att_ref[pl.ds(BLOCK * b, BLOCK), :] = dot(unperm, out.astype(BF16)).astype(BF16)
        cot = go[pl.ds(BLOCK * b, BLOCK), :]
        delta = jnp.broadcast_to(jnp.sum(cot * out, axis=1, keepdims=True), (BLOCK, BLOCK))
        cot, delta = cot * inverse, delta * inverse
        for l in range(5):
            gg[where[l], :] = group(factors[l] * cot, l)
            dd[where[l], :] = group(factors[l] * delta, l)

    def backward(level, c=0):
        r0, n, ref, k0, m, _ = unit(level, c)
        rows, keys = pl.ds(r0, n), pl.ds(k0, m)
        gb = gg[rows, :].astype(BF16)
        eb = ee[rows, :m]
        shift = jnp.concatenate([dd[rows, :]] * (m // BLOCK), axis=1)
        ds = eb.astype(F32) * (dot(gb, ref[keys, BLOCK:], NT) - shift)
        ds = (ds * scale).astype(BF16)
        dq[rows, :] = dot(ds, ref[keys, :BLOCK])
        return dot(ds, qs[rows, :], TN), dot(eb, gb, TN)

    def sides(parts):
        return ((parts[0], pl.ds(0, BLOCK)), (parts[1], pl.ds(BLOCK, BLOCK)))

    def start_back(level):
        for entry in peers:
            if entry[0] == level:
                when(entry[4], lambda: back_copy(entry).start())

    for part, lanes in sides(backward(1, 0)):
        acc1[pl.ds(0, 384), lanes] = part
    for part, lanes in sides(backward(1, 1)):
        edge[pl.ds(0, 64), lanes] = part[:64]
        bk1[pl.ds(64, 64), lanes] = part[64:128].astype(BF16)
        bk1[pl.ds(128, 256), lanes] = (part[128:] + acc1[pl.ds(0, 256), lanes]).astype(BF16)
        bk1[pl.ds(384, 64), lanes] = acc1[pl.ds(256, 64), lanes].astype(BF16)
        edge[pl.ds(64, 64), lanes] = acc1[pl.ds(320, 64), lanes]
    start_back(1)
    for part, lanes in sides(backward(0, 0)):
        fold = 0.5 * expand(edge[pl.ds(0, 64), lanes], 1)
        bk0[pl.ds(0, 128), lanes] = (part[:128] + fold).astype(BF16)
        acc0[pl.ds(0, 256), lanes] = part[128:]
    for part, lanes in sides(backward(0, 3)):
        acc0[pl.ds(256, 256), lanes] = part[:256]
        fold = 0.5 * expand(edge[pl.ds(64, 64), lanes], 1)
        bk0[pl.ds(128, 128), lanes] = (part[256:] + fold).astype(BF16)
    start_back(0)
    for level in BACK_ORDER:
        for part, lanes in sides(backward(level)):
            outbox[level][:, lanes] = part.astype(BF16)
        start_back(level)
    for part, lanes in sides(backward(0, 1)):
        acc0[pl.ds(0, 384), lanes] += part
    for part, lanes in sides(backward(0, 2)):
        acc0[pl.ds(128, 384), lanes] += part

    chunk = 4 * BLOCK // head_count

    def out_copy(index, src, dst, j):
        to = lax.rem(h + j, head_count)
        n = dst.shape[0]
        return pltpu.make_async_remote_copy(
            src_ref=src.at[pl.ds(pl.multiple_of(to * n, n), n), :],
            dst_ref=dst.at[:, pl.ds(pl.multiple_of(h * BLOCK, BLOCK), BLOCK)],
            send_sem=out_send.at[index, to],
            recv_sem=out_recv.at[index, h],
            device_id={"head": to},
            device_id_type=MESH,
        )

    def out_arrival(index, dst, j):
        frm = lax.rem(h + j, head_count)
        here = dst.at[:, pl.ds(pl.multiple_of(frm * BLOCK, BLOCK), BLOCK)]
        pltpu.make_async_remote_copy(
            src_ref=here, dst_ref=here,
            send_sem=out_send.at[index, frm], recv_sem=out_recv.at[index, frm],
            device_id={"head": h}, device_id_type=MESH,
        ).wait_recv()

    def keep(src, dst):
        dst[:, pl.ds(pl.multiple_of(h * BLOCK, BLOCK), BLOCK)] = src[
            pl.ds(pl.multiple_of(h * dst.shape[0], dst.shape[0]), dst.shape[0]), :
        ]

    for b in range(4):
        total = dq[pl.ds(OFF[4] + 8 * b, 8), :]
        for l in (3, 2, 1, 0):
            total = dq[pl.ds(OFF[l] + (BLOCK >> l) * b, BLOCK >> l), :] + 0.5 * expand(total, 1)
        oq[pl.ds(BLOCK * b, BLOCK), :] = dot(unperm, total.astype(BF16)).astype(BF16)
    for j in range(1, head_count):
        out_copy(0, oq, gq_ref, j).start()
    keep(oq, gq_ref)

    for entry in at_level(1) + at_level(0):
        when(entry[4], lambda: back_arrival(entry))
    for b in range(4):
        sum1 = jnp.zeros((64, WIDE), F32)
        if b > 0:
            sum1 = sum1 + rx1[pl.ds(64 * (3 - b), 64), :].astype(F32)
        if b < 3:
            sum1 = sum1 + rx1[pl.ds(192 + 64 * (2 - b), 64), :].astype(F32)
        total = acc0[pl.ds(BLOCK * b, BLOCK), :] + 0.5 * expand(sum1, 1)
        if b == 0:
            total = total + rx0[pl.ds(0, BLOCK), :].astype(F32)
        if b == 3:
            total = total + rx0[pl.ds(BLOCK, BLOCK), :].astype(F32)
        done = dot(unperm, total.astype(BF16)).astype(BF16)
        ok[pl.ds(BLOCK * b, BLOCK), :] = done[:, :BLOCK]
        ov[pl.ds(BLOCK * b, BLOCK), :] = done[:, BLOCK:]
    for j in range(1, head_count):
        out_copy(1, ok, gk_ref, j).start()
        out_copy(2, ov, gv_ref, j).start()
    keep(ok, gk_ref)
    keep(ov, gv_ref)

    for entry in at_level(2) + at_level(3) + at_level(4):
        when(entry[4], lambda: back_arrival(entry))
    sum4 = sum(rx4[pl.ds(32 * i, 32), :].astype(F32) for i in range(8))
    sum3 = sum(rx3[pl.ds(64 * i, 64), :].astype(F32) for i in range(6)) + 0.5 * expand(sum4, 1)
    sum2 = sum(rx2[pl.ds(128 * i, 128), :].astype(F32) for i in range(3)) + 0.5 * expand(sum3, 1)
    r64, c64 = row[:64, :64], col[:64, :64]
    nth = 8 * (r64 >> 4) + (r64 & 7)
    pick = jnp.where(
        c64 == 32 * ((r64 >> 3) & 1) + 8 * (nth & 3) + (nth >> 2), 1.0, 0.0
    ).astype(BF16)
    for b in range(4):
        part = sum2[32 * b : 32 * b + 32]
        part = jnp.concatenate([part[:, :BLOCK], part[:, BLOCK:]], axis=0).astype(BF16)
        oc[pl.ds(64 * b, 64), :] = dot(pick, part).astype(BF16)
    for j in range(1, head_count):
        out_copy(3, oc, coarse, j).start()
    keep(oc, coarse)
    for entry in peers:
        when(entry[4], lambda: (forward_copy(entry).wait_send(), back_copy(entry).wait_send()) and None)
    for index, src, dst in ((0, oq, gq_ref), (1, ok, gk_ref), (2, ov, gv_ref), (3, oc, coarse)):
        for j in range(1, head_count):
            out_copy(index, src, dst, j).wait_send()
            out_arrival(index, dst, j)
    r16, c16 = row[:64, :16], col[:64, :16]
    spread = jnp.where(c16 == 8 * (r16 >> 5) + ((r16 & 31) >> 2), 0.25, 0.0).astype(BF16)
    more = dot(spread, coarse[...])
    gk_ref[...] = (gk_ref[...].astype(F32) + more[:chunk]).astype(BF16)
    gv_ref[...] = (gv_ref[...].astype(F32) + more[chunk:]).astype(BF16)


def write_out(a, b, c, d, a_out, b_out, c_out, d_out, sem):
    copies = [
        pltpu.make_async_copy(src, dst, sem.at[i])
        for i, (src, dst) in enumerate(((a, a_out), (b, b_out), (c, c_out), (d, d_out)))
    ]
    for copy in copies:
        copy.start()
    for copy in copies:
        copy.wait()


def solution(mesh):
    seq_count, head_count = mesh.shape["seq"], mesh.shape["head"]

    def step(queries, keys, values, grad_out):
        rows, width = queries.shape
        vmem = pl.BlockSpec(memory_space=pltpu.VMEM)
        grad = jax.ShapeDtypeStruct((rows // head_count, width * head_count), BF16)

        def wide(n, dtype=BF16):
            return pltpu.VMEM((n, WIDE), dtype)

        def stacked(dtype, width=BLOCK):
            return pltpu.VMEM((STACK, width), dtype)

        sems = pltpu.SemaphoreType.DMA
        results = pl.pallas_call(
            functools.partial(kernel, seq_count, head_count),
            out_shape=(jax.ShapeDtypeStruct((rows, width), BF16), grad, grad, grad),
            in_specs=[pl.BlockSpec(memory_space=pltpu.HBM)] * 4,
            out_specs=(vmem,) * 4,
            scratch_shapes=[
                wide(768), wide(256), wide(128), wide(64), wide(32),
                wide(512), wide(384), wide(384), wide(256),
                stacked(BF16), pltpu.VMEM((rows, width), F32), stacked(BF16, 384),
                stacked(F32), stacked(F32), stacked(F32), stacked(F32), stacked(F32), stacked(F32),
                wide(512, F32), wide(384, F32), wide(128, F32),
                wide(256), wide(512), wide(384), wide(384), wide(256),
                wide(256), wide(384), wide(384), wide(384), wide(256),
                *[pltpu.VMEM((rows, width), BF16) for _ in range(3)],
                pltpu.VMEM((256, BLOCK), BF16), pltpu.VMEM((16, width * head_count), BF16),
                *[pltpu.VMEM((rows, width), BF16) for _ in range(4)],
                sems((4,)),
                sems((SLOTS,)), sems((SLOTS,)), sems((SLOTS,)), sems((SLOTS,)),
                sems((4, head_count)), sems((4, head_count)),
            ],
            compiler_params=pltpu.CompilerParams(
                collective_id=0, has_side_effects=True, vmem_limit_bytes=56000000
            ),
        )(queries, keys, values, grad_out)
        return pl.pallas_call(
            write_out,
            out_shape=tuple(jax.ShapeDtypeStruct(r.shape, r.dtype) for r in results),
            in_specs=[vmem] * 4,
            out_specs=(pl.BlockSpec(memory_space=pltpu.HBM),) * 4,
            scratch_shapes=[sems((4,))],
            compiler_params=pltpu.CompilerParams(vmem_limit_bytes=1024 * 1024),
        )(*results)

    return jax.shard_map(
        step,
        mesh=mesh,
        in_specs=(P("seq", "head"),) * 4,
        out_specs=(P("seq", "head"),) + (P(("seq", "head"), None),) * 3,
        check_vma=False,
    )
```

```python
import functools

import jax
import jax.numpy as jnp
from jax import lax
from jax.experimental import pallas as pl
from jax.experimental.pallas import tpu as pltpu
from jax.sharding import PartitionSpec as P

BLOCK = 128
WIDE = 256
NEG = -1e30
F32 = jnp.float32
BF16 = jnp.bfloat16
LOG2E = 1.4426950408889634
MESH = pl.DeviceIdType.MESH
OUT_SEM = (0, 2, 4, 7, 13)
OUT_SLOTS = 21
OUT_ROWS = (128, 192, 128, 64, 32)
OFF = (0, 512, 768, 896, 960)
STACK = 992
SEM = (0, 2, 4, 7, 10)
ROW_SEM = 12
SLOTS = 16
ROWS = (128, 192, 128, 128, 128)

SEND_ORDER = (0, 1, 4, 3, 2)
FAR_FIRST = (8, 7, 9, 6, 10, 5, 11, 4, 12, 3, 13, 2, 14, 1, 15)
NN = (((1,), (0,)), ((), ()))
NT = (((1,), (1,)), ((), ()))
TN = (((0,), (0,)), ((), ()))


def dot(a, b, dims=NN):
    return lax.dot_general(a, b, dims, preferred_element_type=F32)


def halve(x):
    n, w = x.shape
    x = x.reshape(n // 16, 2, 8, w)
    m = (x[:, 0] + x[:, 1]) * 0.5
    return m.astype(BF16).astype(F32).reshape(n // 2, w)


def expand(x, level):
    n, w = x.shape
    if level == 0:
        return x
    x = x.reshape(n // 8, 1, 8, w)
    x = jnp.broadcast_to(x, (n // 8, 1 << level, 8, w))
    return x.reshape(n << level, w)


def group(x, level):
    n, w = x.shape
    if level == 0:
        return x
    return x.reshape(n >> (level + 3), 1 << level, 8, w).sum(axis=1).reshape(n >> level, w)


def peers_of(s, seq_count):
    out = []

    def both(level, peer, slot, there, ok):
        out.append((level, peer, slot, there, ok, peer, ok))

    y, x = lax.div(s, 4), lax.rem(s, 4)
    up, down = lax.rem(s + seq_count - 4, seq_count), lax.rem(s + 4, seq_count)
    up_ok, down_ok = y > 0, y < 3
    right = x >= 2
    both(4, lax.rem(s + 8, seq_count), 0, 0, None)
    both(4, (3 - y) * 4 + x, 1, 1, (y == 0) | (y == 3))
    both(3, up, 0, 1, up_ok)
    both(3, down, 1, 0, down_ok)
    out.append((
        3, jnp.where(right, down, up), 2, 2,
        (right & down_ok) | (jnp.logical_not(right) & up_ok),
        jnp.where(right, up, down), (right & up_ok) | (jnp.logical_not(right) & down_ok),
    ))
    turn = 3 - 6 * lax.rem(s, 2)
    far = lax.rem(s + seq_count + turn, seq_count)
    both(2, far, 2, 2, (s + turn >= 0) & (s + turn < seq_count))
    both(2, lax.rem(s + seq_count - 2, seq_count), 0, 1, s >= 2)
    both(2, lax.rem(s + 2, seq_count), 1, 0, s + 2 < seq_count)
    prev, after = lax.rem(s + seq_count - 1, seq_count), lax.rem(s + 1, seq_count)
    for level in (1, 0):
        both(level, prev, 0, 1, s > 0)
        both(level, after, 1, 0, s + 1 < seq_count)
    return out


def direct_of(s, seq_count):
    out = []

    def both(level, peer, slot, there, ok):
        out.append((level, peer, slot, there, ok, peer, ok))

    a, e = lax.div(s, 2), lax.rem(s, 2)
    y, x = lax.div(s, 4), lax.rem(s, 4)
    blocks = seq_count // 2
    for f in range(4):
        both(4, lax.rem(y + 2, 4) * 4 + f, f, x, None)
    for f in range(4):
        both(4, (3 - y) * 4 + f, 4 + f, 4 + x, (y == 0) | (y == 3))
    turn = 3 - 6 * lax.rem(a, 2)
    far = lax.rem(a + blocks + turn, blocks)
    for f in range(2):
        both(3, far * 2 + f, 4 + f, 4 + e, (a + turn >= 0) & (a + turn < blocks))
    for f in range(2):
        both(3, lax.rem(a + blocks - 2, blocks) * 2 + f, f, 2 + e, a >= 2)
        both(3, lax.rem(a + 2, blocks) * 2 + f, 2 + f, e, a + 2 < blocks)
    return out


def when(ok, act):
    if ok is None:
        act()
    else:
        pl.when(ok)(act)


def kernel(
    seq_count, head_count,
    q_hbm, k_hbm, v_hbm, g_hbm,
    att_ref, gq_ref, gk_ref, gv_ref,
    kv0, kv1, kv2, kv3, kv4, in1, in2, in3, in4,
    qs, go, ee, pk, tot, sm, gg, dd, dq,
    acc0, acc1, edge, bk0, bk1, bk2, bk3, bk4, rx0, rx1, rx2, rx3, rx4,
    panel, cots, parts, oq, ok, ov, oc, coarse, q_ref, k_ref, v_ref, g_ref, load_sem,
    send_sem, recv_sem, back_send, back_recv, out_send, out_recv,
):
    s, h = lax.axis_index("seq"), lax.axis_index("head")
    barrier = pltpu.get_barrier_semaphore()
    loads = [
        pltpu.make_async_copy(src, dst, load_sem.at[i])
        for i, (src, dst) in enumerate(
            ((k_hbm, k_ref), (v_hbm, v_ref), (q_hbm, q_ref), (g_hbm, g_ref))
        )
    ]
    for load in loads:
        load.start()
    y, x = lax.div(s, 4), lax.rem(s, 4)
    for j in range(1, seq_count):
        pl.semaphore_signal(
            barrier, inc=1, device_id={"seq": lax.rem(s + j, seq_count)}, device_id_type=MESH
        )
    for j in range(1, head_count):
        pl.semaphore_signal(
            barrier, inc=1, device_id={"head": lax.rem(h + j, head_count)}, device_id_type=MESH
        )

    row = lax.broadcasted_iota(jnp.int32, (BLOCK, BLOCK), 0)
    col = lax.broadcasted_iota(jnp.int32, (BLOCK, BLOCK), 1)
    perm = jnp.where(col == (row & 7) * 16 + (row >> 3), 1.0, 0.0).astype(BF16)
    unperm = jnp.where(col == (row & 15) * 8 + (row >> 4), 1.0, 0.0).astype(BF16)

    loads[0].wait()
    loads[1].wait()
    tops = []
    for b in range(4):
        rows = pl.ds(BLOCK * b, BLOCK)
        fine = dot(perm, jnp.concatenate([k_ref[rows, :], v_ref[rows, :]], axis=1))
        kv0[pl.ds(BLOCK + BLOCK * b, BLOCK), :] = fine.astype(BF16)
        m1 = halve(fine)
        kv1[pl.ds(64 * (3 - b), 64), :] = m1.astype(BF16)
        m2 = halve(m1)
        kv2[pl.ds(32 * b, 32), :] = m2.astype(BF16)
        m3 = halve(m2)
        kv3[pl.ds(16 * b, 16), :] = m3.astype(BF16)
        tops.append(halve(m3))
    kv4[...] = jnp.concatenate(tops, axis=0).astype(BF16)

    pl.semaphore_wait(barrier, seq_count - 1 + head_count - 1)

    peers = peers_of(s, seq_count)
    outward = [entry for entry in peers if entry[0] < 3] + direct_of(s, seq_count)
    inbox = (kv0, in1, in2, in3, in4)
    outbox = (bk0, bk1, bk2, bk3, bk4)
    rxbox = (rx0, rx1, rx2, rx3, rx4)

    right = lax.div(x, 2)

    def at_slot(ref, level, slot):
        n = ROWS[level]
        return ref.at[pl.ds(n * slot, n), :]

    def in_slot(level, slot):
        if level == 0:
            return kv0.at[pl.ds(640 * slot, BLOCK), :]
        if level == 1:
            return in1.at[pl.ds(64 + 192 * slot, 192), :]
        n = OUT_ROWS[level]
        return inbox[level].at[pl.ds(n * slot, n), :]

    def out_slot(level, slot):
        if level == 0:
            return kv0.at[pl.ds(BLOCK + 384 * slot, BLOCK), :]
        if level == 1:
            return kv1.at[pl.ds(64 * slot, 192), :]
        return (kv2, kv3, kv4)[level - 2]

    def forward_copy(entry):
        level, peer, slot, there = entry[:4]
        return pltpu.make_async_remote_copy(
            src_ref=out_slot(level, slot),
            dst_ref=in_slot(level, there),
            send_sem=send_sem.at[OUT_SEM[level] + slot],
            recv_sem=recv_sem.at[OUT_SEM[level] + there],
            device_id={"seq": peer},
            device_id_type=MESH,
        )

    def forward_arrival(entry):
        level, peer, slot = entry[:3]
        here = in_slot(level, slot)
        pltpu.make_async_remote_copy(
            src_ref=here, dst_ref=here,
            send_sem=send_sem.at[OUT_SEM[level] + slot], recv_sem=recv_sem.at[OUT_SEM[level] + slot],
            device_id={"seq": peer}, device_id_type=MESH,
        ).wait_recv()

    def back_slot(level, slot):
        if level == 1:
            return bk1.at[pl.ds(64 + 192 * slot, 192), :]
        return at_slot(outbox[level], level, slot)

    def back_copy(entry):
        level, _, slot, there, _, peer, _ = entry
        return pltpu.make_async_remote_copy(
            src_ref=back_slot(level, slot),
            dst_ref=at_slot(rxbox[level], level, there),
            send_sem=back_send.at[SEM[level] + slot],
            recv_sem=back_recv.at[SEM[level] + there],
            device_id={"seq": peer},
            device_id_type=MESH,
        )

    def back_arrival(entry):
        level, peer, slot = entry[:3]
        here = at_slot(rxbox[level], level, slot)
        pltpu.make_async_remote_copy(
            src_ref=here, dst_ref=here,
            send_sem=back_send.at[SEM[level] + slot], recv_sem=back_recv.at[SEM[level] + slot],
            device_id={"seq": peer}, device_id_type=MESH,
        ).wait_recv()

    def at_level(level):
        return [entry for entry in peers if entry[0] == level]

    def row_copy(src, dst, sends, recvs, d):
        to = lax.rem(x + d, 4)
        return pltpu.make_async_remote_copy(
            src_ref=src(to),
            dst_ref=dst.at[pl.ds(pl.multiple_of(x * 64, 64), 64), :],
            send_sem=sends.at[ROW_SEM + to],
            recv_sem=recvs.at[ROW_SEM + x],
            device_id={"seq": y * 4 + to},
            device_id_type=MESH,
        )

    def row_arrival(dst, sends, recvs, d):
        frm = lax.rem(x + d, 4)
        here = dst.at[pl.ds(pl.multiple_of(frm * 64, 64), 64), :]
        pltpu.make_async_remote_copy(
            src_ref=here, dst_ref=here,
            send_sem=sends.at[ROW_SEM + frm], recv_sem=recvs.at[ROW_SEM + frm],
            device_id={"seq": y * 4 + frm}, device_id_type=MESH,
        ).wait_recv()

    def piece_back(d):
        return row_copy(
            lambda to: cots.at[pl.ds(pl.multiple_of(to * 64, 64), 64), :],
            parts, back_send, back_recv, d,
        )

    def out_level(level):
        return [entry for entry in outward if entry[0] == level]

    for level in SEND_ORDER:
        for entry in out_level(level):
            when(entry[4], lambda: forward_copy(entry).start())

    def clear(ref):
        ref[...] = jnp.zeros(ref.shape, BF16)

    for entry in outward:
        if entry[6] is not None:
            when(jnp.logical_not(entry[6]), lambda: clear(in_slot(entry[0], entry[2])))
    for entry in peers:
        if entry[4] is not None:
            when(
                jnp.logical_not(entry[4]),
                lambda: clear(at_slot(rxbox[entry[0]], entry[0], entry[2])),
            )

    loads[2].wait()
    loads[3].wait()
    tops = []
    for b in range(4):
        rows = pl.ds(BLOCK * b, BLOCK)
        both = dot(perm, jnp.concatenate([q_ref[rows, :], g_ref[rows, :]], axis=1))
        go[rows, :] = both[:, BLOCK:]
        fine = both[:, :BLOCK]
        qs[rows, :] = fine.astype(BF16)
        m1 = halve(fine)
        qs[pl.ds(OFF[1] + 64 * b, 64), :] = m1.astype(BF16)
        m2 = halve(m1)
        qs[pl.ds(OFF[2] + 32 * b, 32), :] = m2.astype(BF16)
        m3 = halve(m2)
        qs[pl.ds(OFF[3] + 16 * b, 16), :] = m3.astype(BF16)
        tops.append(halve(m3))
    qs[pl.ds(OFF[4], 32), :] = jnp.concatenate(tops, axis=0).astype(BF16)

    scale = BLOCK ** (-0.5)
    lane = lax.broadcasted_iota(jnp.int32, (8, 384), 1)

    def off_if(bad):
        return jnp.where(bad, NEG, 0.0).astype(F32)

    no_prev, no_next = off_if(s == 0), off_if(s == seq_count - 1)
    a = lax.div(s, 2)

    def thirds(first, second, last):
        return jnp.where(lane < 128, first, jnp.where(lane < 256, second, last))[:1]

    def slot_bias(i, n):
        even = lax.rem(i, 2) == 0
        return thirds(
            off_if(i < 2), off_if(i + 2 > n - 1),
            off_if((even & (i + 3 > n - 1)) | (jnp.logical_not(even) & (i < 3))),
        )

    bias1 = (
        thirds(no_prev, no_next, no_next),
        thirds(no_prev, no_prev, no_next),
    )
    bias2 = slot_bias(s, seq_count)
    bias3 = slot_bias(a, seq_count // 2)
    bias4 = thirds(jnp.zeros((), F32), off_if((y == 1) | (y == 2)), jnp.zeros((), F32))[:, :256]

    def unit(level, c):
        if level == 0:
            bias = {0: thirds(no_prev, 0.0, 0.0), 3: thirds(0.0, 0.0, no_next)}.get(c)
            return (OFF[0] + BLOCK * c, BLOCK, kv0, BLOCK * c, 384, bias)
        if level == 1:
            return (OFF[1] + BLOCK * c, BLOCK, in1, BLOCK * (1 - c), 384, bias1[c])
        if level == 2:
            return (OFF[2], 128, in2, 0, 384, bias2)
        if level == 3:
            return (OFF[3], 64, in3, 0, 384, bias3)
        return (OFF[4], 32, in4, 0, 256, bias4)

    def forward(level, c=0):
        r0, n, ref, k0, m, bias = unit(level, c)
        rows, keys = pl.ds(r0, n), pl.ds(k0, m)
        sc = dot(qs[rows, :], ref[keys, :BLOCK], NT) * (scale * LOG2E)
        if bias is not None:
            sc = sc + bias
        top = jnp.max(sc, axis=1, keepdims=True)
        e = jnp.exp2(sc - top)
        pk[rows, :] = jnp.broadcast_to(top, (n, BLOCK))
        tot[rows, :] = jnp.broadcast_to(jnp.sum(e, axis=1, keepdims=True), (n, BLOCK))
        eb = e.astype(BF16)
        ee[rows, :m] = eb
        sm[rows, :] = dot(eb, ref[keys, BLOCK:])

    forward(0, 1)
    forward(0, 2)
    for level in SEND_ORDER:
        for entry in out_level(level):
            when(entry[6], lambda: forward_arrival(entry))
        if level == 0:
            in1[pl.ds(0, 64), :] = halve(kv0[pl.ds(0, BLOCK), :].astype(F32)).astype(BF16)
            in1[pl.ds(448, 64), :] = halve(kv0[pl.ds(640, BLOCK), :].astype(F32)).astype(BF16)
            forward(0, 0)
            forward(0, 3)
        elif level == 1:
            forward(1, 0)
            forward(1, 1)
        else:
            forward(level)

    for b in range(4):
        where = [pl.ds(OFF[l] + (BLOCK >> l) * b, BLOCK >> l) for l in range(5)]
        peaks = [expand(pk[where[l], :], l) for l in range(5)]
        overall = functools.reduce(jnp.maximum, peaks)
        factors = [jnp.exp2(peaks[l] - overall) * float(1 << l) for l in range(5)]
        den = sum(factors[l] * expand(tot[where[l], :], l) for l in range(5))
        num = sum(factors[l] * expand(sm[where[l], :], l) for l in range(5))
        inverse = 1.0 / den
        out = num * inverse
        att_ref[pl.ds(BLOCK * b, BLOCK), :] = dot(unperm, out.astype(BF16)).astype(BF16)
        cot = go[pl.ds(BLOCK * b, BLOCK), :]
        delta = jnp.broadcast_to(jnp.sum(cot * out, axis=1, keepdims=True), (BLOCK, BLOCK))
        cot, delta = cot * inverse, delta * inverse
        for l in range(5):
            gg[where[l], :] = group(factors[l] * cot, l)
            dd[where[l], :] = group(factors[l] * delta, l)

    def backward(level, c=0):
        r0, n, ref, k0, m, _ = unit(level, c)
        rows, keys = pl.ds(r0, n), pl.ds(k0, m)
        gb = gg[rows, :].astype(BF16)
        eb = ee[rows, :m]
        shift = jnp.concatenate([dd[rows, :]] * (m // BLOCK), axis=1)
        ds = eb.astype(F32) * (dot(gb, ref[keys, BLOCK:], NT) - shift)
        ds = (ds * scale).astype(BF16)
        dq[rows, :] = dot(ds, ref[keys, :BLOCK])
        return dot(ds, qs[rows, :], TN), dot(eb, gb, TN)

    def sides(parts):
        return ((parts[0], pl.ds(0, BLOCK)), (parts[1], pl.ds(BLOCK, BLOCK)))

    def start_back(level):
        for entry in peers:
            if entry[0] == level:
                when(entry[6], lambda: back_copy(entry).start())

    for level in (4, 3):
        for part, lanes in sides(backward(level)):
            outbox[level][:, lanes] = part.astype(BF16)
        start_back(level)
    for part, lanes in sides(backward(1, 0)):
        acc1[pl.ds(0, 384), lanes] = part
    for part, lanes in sides(backward(1, 1)):
        edge[pl.ds(0, 64), lanes] = part[:64]
        bk1[pl.ds(64, 64), lanes] = part[64:128].astype(BF16)
        bk1[pl.ds(128, 256), lanes] = (part[128:] + acc1[pl.ds(0, 256), lanes]).astype(BF16)
        bk1[pl.ds(384, 64), lanes] = acc1[pl.ds(256, 64), lanes].astype(BF16)
        edge[pl.ds(64, 64), lanes] = acc1[pl.ds(320, 64), lanes]
    start_back(1)
    for part, lanes in sides(backward(0, 0)):
        fold = 0.5 * expand(edge[pl.ds(0, 64), lanes], 1)
        bk0[pl.ds(0, 128), lanes] = (part[:128] + fold).astype(BF16)
        acc0[pl.ds(0, 256), lanes] = part[128:]
    for part, lanes in sides(backward(0, 3)):
        acc0[pl.ds(256, 256), lanes] = part[:256]
        fold = 0.5 * expand(edge[pl.ds(64, 64), lanes], 1)
        bk0[pl.ds(128, 128), lanes] = (part[256:] + fold).astype(BF16)
    start_back(0)
    for level in (2,):
        for part, lanes in sides(backward(level)):
            outbox[level][:, lanes] = part.astype(BF16)
        start_back(level)
    for part, lanes in sides(backward(0, 1)):
        acc0[pl.ds(0, 384), lanes] += part
    for part, lanes in sides(backward(0, 2)):
        acc0[pl.ds(128, 384), lanes] += part

    chunk = 4 * BLOCK // head_count

    def out_copy(index, src, dst, j):
        to = lax.rem(h + j, head_count)
        n = dst.shape[0]
        return pltpu.make_async_remote_copy(
            src_ref=src.at[pl.ds(pl.multiple_of(to * n, n), n), :],
            dst_ref=dst.at[:, pl.ds(pl.multiple_of(h * BLOCK, BLOCK), BLOCK)],
            send_sem=out_send.at[index, to],
            recv_sem=out_recv.at[index, h],
            device_id={"head": to},
            device_id_type=MESH,
        )

    def out_arrival(index, dst, j):
        frm = lax.rem(h + j, head_count)
        here = dst.at[:, pl.ds(pl.multiple_of(frm * BLOCK, BLOCK), BLOCK)]
        pltpu.make_async_remote_copy(
            src_ref=here, dst_ref=here,
            send_sem=out_send.at[index, frm], recv_sem=out_recv.at[index, frm],
            device_id={"head": h}, device_id_type=MESH,
        ).wait_recv()

    def keep(src, dst):
        dst[:, pl.ds(pl.multiple_of(h * BLOCK, BLOCK), BLOCK)] = src[
            pl.ds(pl.multiple_of(h * dst.shape[0], dst.shape[0]), dst.shape[0]), :
        ]

    for b in range(4):
        total = dq[pl.ds(OFF[4] + 8 * b, 8), :]
        for l in (3, 2, 1, 0):
            total = dq[pl.ds(OFF[l] + (BLOCK >> l) * b, BLOCK >> l), :] + 0.5 * expand(total, 1)
        oq[pl.ds(BLOCK * b, BLOCK), :] = dot(unperm, total.astype(BF16)).astype(BF16)
    for j in FAR_FIRST:
        out_copy(0, oq, gq_ref, j).start()
    keep(oq, gq_ref)

    for entry in at_level(4) + at_level(3):
        when(entry[4], lambda: back_arrival(entry))
    sum4 = rx4[pl.ds(0, BLOCK), :].astype(F32) + rx4[pl.ds(BLOCK, BLOCK), :].astype(F32)
    panel[...] = 0.5 * expand(sum4, 1)
    near_rows = pl.ds(pl.multiple_of(right * BLOCK, BLOCK), BLOCK)
    far_rows = pl.ds(pl.multiple_of((1 - right) * BLOCK, BLOCK), BLOCK)
    panel[near_rows, :] += rx3[pl.ds(0, BLOCK), :].astype(F32) + rx3[pl.ds(BLOCK, BLOCK), :].astype(F32)
    panel[far_rows, :] += rx3[pl.ds(2 * BLOCK, BLOCK), :].astype(F32)
    cots[...] = panel[...].astype(BF16)
    for d in (2, 1, 3):
        piece_back(d).start()

    for entry in at_level(1) + at_level(0):
        when(entry[4], lambda: back_arrival(entry))
    for b in range(4):
        sum1 = jnp.zeros((64, WIDE), F32)
        if b > 0:
            sum1 = sum1 + rx1[pl.ds(64 * (3 - b), 64), :].astype(F32)
        if b < 3:
            sum1 = sum1 + rx1[pl.ds(192 + 64 * (2 - b), 64), :].astype(F32)
        total = acc0[pl.ds(BLOCK * b, BLOCK), :] + 0.5 * expand(sum1, 1)
        if b == 0:
            total = total + rx0[pl.ds(0, BLOCK), :].astype(F32)
        if b == 3:
            total = total + rx0[pl.ds(BLOCK, BLOCK), :].astype(F32)
        done = dot(unperm, total.astype(BF16)).astype(BF16)
        ok[pl.ds(BLOCK * b, BLOCK), :] = done[:, :BLOCK]
        ov[pl.ds(BLOCK * b, BLOCK), :] = done[:, BLOCK:]
    for j in FAR_FIRST:
        out_copy(1, ok, gk_ref, j).start()
        out_copy(2, ov, gv_ref, j).start()
    keep(ok, gk_ref)
    keep(ov, gv_ref)

    for entry in at_level(2):
        when(entry[4], lambda: back_arrival(entry))
    sum3 = panel[pl.ds(pl.multiple_of(x * 64, 64), 64), :]
    for d in (1, 2, 3):
        row_arrival(parts, back_send, back_recv, d)
        frm = lax.rem(x + d, 4)
        sum3 = sum3 + parts[pl.ds(pl.multiple_of(frm * 64, 64), 64), :].astype(F32)
    sum2 = sum(rx2[pl.ds(128 * i, 128), :].astype(F32) for i in range(3)) + 0.5 * expand(sum3, 1)
    r64, c64 = row[:64, :64], col[:64, :64]
    nth = 8 * (r64 >> 4) + (r64 & 7)
    pick = jnp.where(
        c64 == 32 * ((r64 >> 3) & 1) + 8 * (nth & 3) + (nth >> 2), 1.0, 0.0
    ).astype(BF16)
    for b in range(4):
        part = sum2[32 * b : 32 * b + 32]
        part = jnp.concatenate([part[:, :BLOCK], part[:, BLOCK:]], axis=0).astype(BF16)
        oc[pl.ds(64 * b, 64), :] = dot(pick, part).astype(BF16)
    for j in FAR_FIRST:
        out_copy(3, oc, coarse, j).start()
    keep(oc, coarse)
    for entry in peers:
        when(entry[6], lambda: back_copy(entry).wait_send())
    for entry in outward:
        when(entry[4], lambda: forward_copy(entry).wait_send())
    for d in (1, 2, 3):
        piece_back(d).wait_send()
    for index, src, dst in ((0, oq, gq_ref), (1, ok, gk_ref), (2, ov, gv_ref), (3, oc, coarse)):
        for j in range(1, head_count):
            out_copy(index, src, dst, j).wait_send()
            out_arrival(index, dst, j)
    r16, c16 = row[:64, :16], col[:64, :16]
    spread = jnp.where(c16 == 8 * (r16 >> 5) + ((r16 & 31) >> 2), 0.25, 0.0).astype(BF16)
    more = dot(spread, coarse[...])
    gk_ref[...] = (gk_ref[...].astype(F32) + more[:chunk]).astype(BF16)
    gv_ref[...] = (gv_ref[...].astype(F32) + more[chunk:]).astype(BF16)


def write_out(a, b, c, d, a_out, b_out, c_out, d_out, sem):
    copies = [
        pltpu.make_async_copy(src, dst, sem.at[i])
        for i, (src, dst) in enumerate(((a, a_out), (b, b_out), (c, c_out), (d, d_out)))
    ]
    for copy in copies:
        copy.start()
    for copy in copies:
        copy.wait()


def solution(mesh):
    seq_count, head_count = mesh.shape["seq"], mesh.shape["head"]

    def step(queries, keys, values, grad_out):
        rows, width = queries.shape
        vmem = pl.BlockSpec(memory_space=pltpu.VMEM)
        grad = jax.ShapeDtypeStruct((rows // head_count, width * head_count), BF16)

        def wide(n, dtype=BF16):
            return pltpu.VMEM((n, WIDE), dtype)

        def stacked(dtype, width=BLOCK):
            return pltpu.VMEM((STACK, width), dtype)

        sems = pltpu.SemaphoreType.DMA
        results = pl.pallas_call(
            functools.partial(kernel, seq_count, head_count),
            out_shape=(jax.ShapeDtypeStruct((rows, width), BF16), grad, grad, grad),
            in_specs=[pl.BlockSpec(memory_space=pltpu.HBM)] * 4,
            out_specs=(vmem,) * 4,
            scratch_shapes=[
                wide(768), wide(256), wide(128), wide(64), wide(32),
                wide(512), wide(384), wide(384), wide(256),
                stacked(BF16), pltpu.VMEM((rows, width), F32), stacked(BF16, 384),
                stacked(F32), stacked(F32), stacked(F32), stacked(F32), stacked(F32), stacked(F32),
                wide(512, F32), wide(384, F32), wide(128, F32),
                wide(256), wide(512), wide(384), wide(384), wide(256),
                wide(256), wide(384), wide(384), wide(384), wide(256),
                wide(256, F32), wide(256), wide(256),
                *[pltpu.VMEM((rows, width), BF16) for _ in range(3)],
                pltpu.VMEM((256, BLOCK), BF16), pltpu.VMEM((16, width * head_count), BF16),
                *[pltpu.VMEM((rows, width), BF16) for _ in range(4)],
                sems((4,)),
                sems((OUT_SLOTS,)), sems((OUT_SLOTS,)), sems((SLOTS,)), sems((SLOTS,)),
                sems((4, head_count)), sems((4, head_count)),
            ],
            compiler_params=pltpu.CompilerParams(
                collective_id=0, has_side_effects=True, vmem_limit_bytes=56000000
            ),
        )(queries, keys, values, grad_out)
        return pl.pallas_call(
            write_out,
            out_shape=tuple(jax.ShapeDtypeStruct(r.shape, r.dtype) for r in results),
            in_specs=[vmem] * 4,
            out_specs=(pl.BlockSpec(memory_space=pltpu.HBM),) * 4,
            scratch_shapes=[sems((4,))],
            compiler_params=pltpu.CompilerParams(vmem_limit_bytes=1024 * 1024),
        )(*results)

    return jax.shard_map(
        step,
        mesh=mesh,
        in_specs=(P("seq", "head"),) * 4,
        out_specs=(P("seq", "head"),) + (P(("seq", "head"), None),) * 3,
        check_vma=False,
    )
```

```python
import functools

import jax
import jax.numpy as jnp
from jax import lax
from jax.experimental import pallas as pl
from jax.experimental.pallas import tpu as pltpu
from jax.sharding import PartitionSpec as P

BLOCK = 128
WIDE = 256
NEG = -1e30
F32 = jnp.float32
BF16 = jnp.bfloat16
LOG2E = 1.4426950408889634
MESH = pl.DeviceIdType.MESH
OUT_SEM = (0, 2, 4, 7, 13)
OUT_SLOTS = 21
OUT_ROWS = (128, 192, 128, 64, 32)
OFF = (0, 512, 768, 896, 960)
STACK = 992
SEM = (0, 2, 4, 7, 10)
ROW_SEM = 12
SLOTS = 16
ROWS = (128, 192, 128, 128, 128)

SEND_ORDER = (0, 1, 4, 3, 2)
FIRST_FAR = 4
FAR_FIRST = (8, 7, 9, 6, 10, 5, 11, 4, 12, 3, 13, 2, 14, 1, 15)
NN = (((1,), (0,)), ((), ()))
NT = (((1,), (1,)), ((), ()))
TN = (((0,), (0,)), ((), ()))


def dot(a, b, dims=NN):
    return lax.dot_general(a, b, dims, preferred_element_type=F32)


def halve(x):
    n, w = x.shape
    x = x.reshape(n // 16, 2, 8, w)
    m = (x[:, 0] + x[:, 1]) * 0.5
    return m.astype(BF16).astype(F32).reshape(n // 2, w)


def expand(x, level):
    n, w = x.shape
    if level == 0:
        return x
    x = x.reshape(n // 8, 1, 8, w)
    x = jnp.broadcast_to(x, (n // 8, 1 << level, 8, w))
    return x.reshape(n << level, w)


def group(x, level):
    n, w = x.shape
    if level == 0:
        return x
    return x.reshape(n >> (level + 3), 1 << level, 8, w).sum(axis=1).reshape(n >> level, w)


def peers_of(s, seq_count):
    out = []

    def both(level, peer, slot, there, ok):
        out.append((level, peer, slot, there, ok, peer, ok))

    y, x = lax.div(s, 4), lax.rem(s, 4)
    up, down = lax.rem(s + seq_count - 4, seq_count), lax.rem(s + 4, seq_count)
    up_ok, down_ok = y > 0, y < 3
    right = x >= 2
    both(4, lax.rem(s + 8, seq_count), 0, 0, None)
    both(4, (3 - y) * 4 + x, 1, 1, (y == 0) | (y == 3))
    both(3, up, 0, 1, up_ok)
    both(3, down, 1, 0, down_ok)
    out.append((
        3, jnp.where(right, down, up), 2, 2,
        (right & down_ok) | (jnp.logical_not(right) & up_ok),
        jnp.where(right, up, down), (right & up_ok) | (jnp.logical_not(right) & down_ok),
    ))
    turn = 3 - 6 * lax.rem(s, 2)
    far = lax.rem(s + seq_count + turn, seq_count)
    both(2, far, 2, 2, (s + turn >= 0) & (s + turn < seq_count))
    both(2, lax.rem(s + seq_count - 2, seq_count), 0, 1, s >= 2)
    both(2, lax.rem(s + 2, seq_count), 1, 0, s + 2 < seq_count)
    prev, after = lax.rem(s + seq_count - 1, seq_count), lax.rem(s + 1, seq_count)
    for level in (1, 0):
        both(level, prev, 0, 1, s > 0)
        both(level, after, 1, 0, s + 1 < seq_count)
    return out


def direct_of(s, seq_count):
    out = []

    def both(level, peer, slot, there, ok):
        out.append((level, peer, slot, there, ok, peer, ok))

    a, e = lax.div(s, 2), lax.rem(s, 2)
    y, x = lax.div(s, 4), lax.rem(s, 4)
    blocks = seq_count // 2
    for f in range(4):
        both(4, lax.rem(y + 2, 4) * 4 + f, f, x, None)
    for f in range(4):
        both(4, (3 - y) * 4 + f, 4 + f, 4 + x, (y == 0) | (y == 3))
    turn = 3 - 6 * lax.rem(a, 2)
    far = lax.rem(a + blocks + turn, blocks)
    for f in range(2):
        both(3, far * 2 + f, 4 + f, 4 + e, (a + turn >= 0) & (a + turn < blocks))
    for f in range(2):
        both(3, lax.rem(a + blocks - 2, blocks) * 2 + f, f, 2 + e, a >= 2)
        both(3, lax.rem(a + 2, blocks) * 2 + f, 2 + f, e, a + 2 < blocks)
    return out


def when(ok, act):
    if ok is None:
        act()
    else:
        pl.when(ok)(act)


def kernel(
    seq_count, head_count,
    q_hbm, k_hbm, v_hbm, g_hbm,
    att_ref, gq_ref, gk_ref, gv_ref,
    kv0, kv1, kv2, kv3, kv4, in1, in2, in3, in4,
    qs, go, ee, pk, tot, sm, gg, dd, dq,
    acc0, acc1, edge, bk0, bk1, bk2, bk3, bk4, rx0, rx1, rx2, rx3, rx4,
    panel, cots, parts, oq, ok, ov, oc, coarse, q_ref, k_ref, v_ref, g_ref, load_sem,
    send_sem, recv_sem, back_send, back_recv, out_send, out_recv, row_sem, chip_sem, core_sem,
):
    s, h = lax.axis_index("seq"), lax.axis_index("head")
    barrier = pltpu.get_barrier_semaphore()
    loads = [
        pltpu.make_async_copy(src, dst, load_sem.at[i])
        for i, (src, dst) in enumerate(
            ((k_hbm, k_ref), (v_hbm, v_ref), (q_hbm, q_ref), (g_hbm, g_ref))
        )
    ]
    for load in loads:
        load.start()
    y, x = lax.div(s, 4), lax.rem(s, 4)
    row_mates = [y * 4 + lax.rem(x + d, 4) for d in (1, 2, 3)]
    near = [lax.rem(s + seq_count + d, seq_count) for d in (-1, 1)] + row_mates
    near += [lax.rem(s + 4 * d, seq_count) for d in (1, 2, 3)]
    core = h + 1 - 2 * lax.rem(h, 2)
    two_away = [lax.rem(h + d, head_count) for d in (4, head_count - 4)]
    near_head = [core] + two_away + [lax.rem(h + d, head_count) for d in (2, head_count - 2)]

    def tell(sem, axis, peers):
        for peer in peers:
            pl.semaphore_signal(sem, inc=1, device_id={axis: peer}, device_id_type=MESH)

    tell(barrier, "seq", near)
    tell(barrier, "head", near_head)

    row = lax.broadcasted_iota(jnp.int32, (BLOCK, BLOCK), 0)
    col = lax.broadcasted_iota(jnp.int32, (BLOCK, BLOCK), 1)
    perm = jnp.where(col == (row & 7) * 16 + (row >> 3), 1.0, 0.0).astype(BF16)
    unperm = jnp.where(col == (row & 15) * 8 + (row >> 4), 1.0, 0.0).astype(BF16)

    loads[0].wait()
    loads[1].wait()
    tops = []
    for b in range(4):
        rows = pl.ds(BLOCK * b, BLOCK)
        fine = dot(perm, jnp.concatenate([k_ref[rows, :], v_ref[rows, :]], axis=1))
        kv0[pl.ds(BLOCK + BLOCK * b, BLOCK), :] = fine.astype(BF16)
        m1 = halve(fine)
        kv1[pl.ds(64 * (3 - b), 64), :] = m1.astype(BF16)
        m2 = halve(m1)
        kv2[pl.ds(32 * b, 32), :] = m2.astype(BF16)
        m3 = halve(m2)
        kv3[pl.ds(16 * b, 16), :] = m3.astype(BF16)
        tops.append(halve(m3))
    kv4[...] = jnp.concatenate(tops, axis=0).astype(BF16)

    pl.semaphore_wait(barrier, len(near) + len(near_head))
    tell(row_sem, "seq", row_mates)
    tell(chip_sem, "head", two_away)

    peers = peers_of(s, seq_count)
    outward = [entry for entry in peers if entry[0] < 3] + direct_of(s, seq_count)
    inbox = (kv0, in1, in2, in3, in4)
    outbox = (bk0, bk1, bk2, bk3, bk4)
    rxbox = (rx0, rx1, rx2, rx3, rx4)

    right = lax.div(x, 2)

    def at_slot(ref, level, slot):
        n = ROWS[level]
        return ref.at[pl.ds(n * slot, n), :]

    def in_slot(level, slot):
        if level == 0:
            return kv0.at[pl.ds(640 * slot, BLOCK), :]
        if level == 1:
            return in1.at[pl.ds(64 + 192 * slot, 192), :]
        n = OUT_ROWS[level]
        return inbox[level].at[pl.ds(n * slot, n), :]

    def out_slot(level, slot):
        if level == 0:
            return kv0.at[pl.ds(BLOCK + 384 * slot, BLOCK), :]
        if level == 1:
            return kv1.at[pl.ds(64 * slot, 192), :]
        return (kv2, kv3, kv4)[level - 2]

    def forward_copy(entry):
        level, peer, slot, there = entry[:4]
        return pltpu.make_async_remote_copy(
            src_ref=out_slot(level, slot),
            dst_ref=in_slot(level, there),
            send_sem=send_sem.at[OUT_SEM[level] + slot],
            recv_sem=recv_sem.at[OUT_SEM[level] + there],
            device_id={"seq": peer},
            device_id_type=MESH,
        )

    def forward_arrival(entry):
        level, peer, slot = entry[:3]
        here = in_slot(level, slot)
        pltpu.make_async_remote_copy(
            src_ref=here, dst_ref=here,
            send_sem=send_sem.at[OUT_SEM[level] + slot], recv_sem=recv_sem.at[OUT_SEM[level] + slot],
            device_id={"seq": peer}, device_id_type=MESH,
        ).wait_recv()

    def back_slot(level, slot):
        if level == 1:
            return bk1.at[pl.ds(64 + 192 * slot, 192), :]
        return at_slot(outbox[level], level, slot)

    def back_copy(entry):
        level, _, slot, there, _, peer, _ = entry
        return pltpu.make_async_remote_copy(
            src_ref=back_slot(level, slot),
            dst_ref=at_slot(rxbox[level], level, there),
            send_sem=back_send.at[SEM[level] + slot],
            recv_sem=back_recv.at[SEM[level] + there],
            device_id={"seq": peer},
            device_id_type=MESH,
        )

    def back_arrival(entry):
        level, peer, slot = entry[:3]
        here = at_slot(rxbox[level], level, slot)
        pltpu.make_async_remote_copy(
            src_ref=here, dst_ref=here,
            send_sem=back_send.at[SEM[level] + slot], recv_sem=back_recv.at[SEM[level] + slot],
            device_id={"seq": peer}, device_id_type=MESH,
        ).wait_recv()

    def at_level(level):
        return [entry for entry in peers if entry[0] == level]

    def row_copy(src, dst, sends, recvs, d):
        to = lax.rem(x + d, 4)
        return pltpu.make_async_remote_copy(
            src_ref=src(to),
            dst_ref=dst.at[pl.ds(pl.multiple_of(x * 64, 64), 64), :],
            send_sem=sends.at[ROW_SEM + to],
            recv_sem=recvs.at[ROW_SEM + x],
            device_id={"seq": y * 4 + to},
            device_id_type=MESH,
        )

    def row_arrival(dst, sends, recvs, d):
        frm = lax.rem(x + d, 4)
        here = dst.at[pl.ds(pl.multiple_of(frm * 64, 64), 64), :]
        pltpu.make_async_remote_copy(
            src_ref=here, dst_ref=here,
            send_sem=sends.at[ROW_SEM + frm], recv_sem=recvs.at[ROW_SEM + frm],
            device_id={"seq": y * 4 + frm}, device_id_type=MESH,
        ).wait_recv()

    def piece_back(d):
        return row_copy(
            lambda to: cots.at[pl.ds(pl.multiple_of(to * 64, 64), 64), :],
            parts, back_send, back_recv, d,
        )

    def out_level(level):
        return [entry for entry in outward if entry[0] == level]

    for level in SEND_ORDER:
        if level == FIRST_FAR:
            pl.semaphore_wait(row_sem, len(row_mates))
        for entry in out_level(level):
            when(entry[4], lambda: forward_copy(entry).start())

    def clear(ref):
        ref[...] = jnp.zeros(ref.shape, BF16)

    for entry in outward:
        if entry[6] is not None:
            when(jnp.logical_not(entry[6]), lambda: clear(in_slot(entry[0], entry[2])))
    for entry in peers:
        if entry[4] is not None:
            when(
                jnp.logical_not(entry[4]),
                lambda: clear(at_slot(rxbox[entry[0]], entry[0], entry[2])),
            )

    loads[2].wait()
    loads[3].wait()
    tops = []
    for b in range(4):
        rows = pl.ds(BLOCK * b, BLOCK)
        both = dot(perm, jnp.concatenate([q_ref[rows, :], g_ref[rows, :]], axis=1))
        go[rows, :] = both[:, BLOCK:]
        fine = both[:, :BLOCK]
        qs[rows, :] = fine.astype(BF16)
        m1 = halve(fine)
        qs[pl.ds(OFF[1] + 64 * b, 64), :] = m1.astype(BF16)
        m2 = halve(m1)
        qs[pl.ds(OFF[2] + 32 * b, 32), :] = m2.astype(BF16)
        m3 = halve(m2)
        qs[pl.ds(OFF[3] + 16 * b, 16), :] = m3.astype(BF16)
        tops.append(halve(m3))
    qs[pl.ds(OFF[4], 32), :] = jnp.concatenate(tops, axis=0).astype(BF16)

    scale = BLOCK ** (-0.5)
    lane = lax.broadcasted_iota(jnp.int32, (8, 384), 1)

    def off_if(bad):
        return jnp.where(bad, NEG, 0.0).astype(F32)

    no_prev, no_next = off_if(s == 0), off_if(s == seq_count - 1)
    a = lax.div(s, 2)

    def thirds(first, second, last):
        return jnp.where(lane < 128, first, jnp.where(lane < 256, second, last))[:1]

    def slot_bias(i, n):
        even = lax.rem(i, 2) == 0
        return thirds(
            off_if(i < 2), off_if(i + 2 > n - 1),
            off_if((even & (i + 3 > n - 1)) | (jnp.logical_not(even) & (i < 3))),
        )

    bias1 = (
        thirds(no_prev, no_next, no_next),
        thirds(no_prev, no_prev, no_next),
    )
    bias2 = slot_bias(s, seq_count)
    bias3 = slot_bias(a, seq_count // 2)
    bias4 = thirds(jnp.zeros((), F32), off_if((y == 1) | (y == 2)), jnp.zeros((), F32))[:, :256]

    def unit(level, c):
        if level == 0:
            bias = {0: thirds(no_prev, 0.0, 0.0), 3: thirds(0.0, 0.0, no_next)}.get(c)
            return (OFF[0] + BLOCK * c, BLOCK, kv0, BLOCK * c, 384, bias)
        if level == 1:
            return (OFF[1] + BLOCK * c, BLOCK, in1, BLOCK * (1 - c), 384, bias1[c])
        if level == 2:
            return (OFF[2], 128, in2, 0, 384, bias2)
        if level == 3:
            return (OFF[3], 64, in3, 0, 384, bias3)
        return (OFF[4], 32, in4, 0, 256, bias4)

    def forward(level, c=0):
        r0, n, ref, k0, m, bias = unit(level, c)
        rows, keys = pl.ds(r0, n), pl.ds(k0, m)
        sc = dot(qs[rows, :], ref[keys, :BLOCK], NT) * (scale * LOG2E)
        if bias is not None:
            sc = sc + bias
        top = jnp.max(sc, axis=1, keepdims=True)
        e = jnp.exp2(sc - top)
        pk[rows, :] = jnp.broadcast_to(top, (n, BLOCK))
        tot[rows, :] = jnp.broadcast_to(jnp.sum(e, axis=1, keepdims=True), (n, BLOCK))
        eb = e.astype(BF16)
        ee[rows, :m] = eb
        sm[rows, :] = dot(eb, ref[keys, BLOCK:])

    forward(0, 1)
    forward(0, 2)
    for level in SEND_ORDER:
        for entry in out_level(level):
            when(entry[6], lambda: forward_arrival(entry))
        if level == 0:
            in1[pl.ds(0, 64), :] = halve(kv0[pl.ds(0, BLOCK), :].astype(F32)).astype(BF16)
            in1[pl.ds(448, 64), :] = halve(kv0[pl.ds(640, BLOCK), :].astype(F32)).astype(BF16)
            forward(0, 0)
            forward(0, 3)
        elif level == 1:
            forward(1, 0)
            forward(1, 1)
        else:
            forward(level)

    pl.semaphore_wait(chip_sem, len(two_away))
    tell(core_sem, "head", [core])

    for b in range(4):
        where = [pl.ds(OFF[l] + (BLOCK >> l) * b, BLOCK >> l) for l in range(5)]
        peaks = [expand(pk[where[l], :], l) for l in range(5)]
        overall = functools.reduce(jnp.maximum, peaks)
        factors = [jnp.exp2(peaks[l] - overall) * float(1 << l) for l in range(5)]
        den = sum(factors[l] * expand(tot[where[l], :], l) for l in range(5))
        num = sum(factors[l] * expand(sm[where[l], :], l) for l in range(5))
        inverse = 1.0 / den
        out = num * inverse
        att_ref[pl.ds(BLOCK * b, BLOCK), :] = dot(unperm, out.astype(BF16)).astype(BF16)
        cot = go[pl.ds(BLOCK * b, BLOCK), :]
        delta = jnp.broadcast_to(jnp.sum(cot * out, axis=1, keepdims=True), (BLOCK, BLOCK))
        cot, delta = cot * inverse, delta * inverse
        for l in range(5):
            gg[where[l], :] = group(factors[l] * cot, l)
            dd[where[l], :] = group(factors[l] * delta, l)

    def backward(level, c=0):
        r0, n, ref, k0, m, _ = unit(level, c)
        rows, keys = pl.ds(r0, n), pl.ds(k0, m)
        gb = gg[rows, :].astype(BF16)
        eb = ee[rows, :m]
        shift = jnp.concatenate([dd[rows, :]] * (m // BLOCK), axis=1)
        ds = eb.astype(F32) * (dot(gb, ref[keys, BLOCK:], NT) - shift)
        ds = (ds * scale).astype(BF16)
        dq[rows, :] = dot(ds, ref[keys, :BLOCK])
        return dot(ds, qs[rows, :], TN), dot(eb, gb, TN)

    def sides(parts):
        return ((parts[0], pl.ds(0, BLOCK)), (parts[1], pl.ds(BLOCK, BLOCK)))

    def start_back(level):
        for entry in peers:
            if entry[0] == level:
                when(entry[6], lambda: back_copy(entry).start())

    for level in (4, 3):
        for part, lanes in sides(backward(level)):
            outbox[level][:, lanes] = part.astype(BF16)
        start_back(level)
    for part, lanes in sides(backward(1, 0)):
        acc1[pl.ds(0, 384), lanes] = part
    for part, lanes in sides(backward(1, 1)):
        edge[pl.ds(0, 64), lanes] = part[:64]
        bk1[pl.ds(64, 64), lanes] = part[64:128].astype(BF16)
        bk1[pl.ds(128, 256), lanes] = (part[128:] + acc1[pl.ds(0, 256), lanes]).astype(BF16)
        bk1[pl.ds(384, 64), lanes] = acc1[pl.ds(256, 64), lanes].astype(BF16)
        edge[pl.ds(64, 64), lanes] = acc1[pl.ds(320, 64), lanes]
    start_back(1)
    for part, lanes in sides(backward(0, 0)):
        fold = 0.5 * expand(edge[pl.ds(0, 64), lanes], 1)
        bk0[pl.ds(0, 128), lanes] = (part[:128] + fold).astype(BF16)
        acc0[pl.ds(0, 256), lanes] = part[128:]
    for part, lanes in sides(backward(0, 3)):
        acc0[pl.ds(256, 256), lanes] = part[:256]
        fold = 0.5 * expand(edge[pl.ds(64, 64), lanes], 1)
        bk0[pl.ds(128, 128), lanes] = (part[256:] + fold).astype(BF16)
    start_back(0)
    for level in (2,):
        for part, lanes in sides(backward(level)):
            outbox[level][:, lanes] = part.astype(BF16)
        start_back(level)
    for part, lanes in sides(backward(0, 1)):
        acc0[pl.ds(0, 384), lanes] += part
    for part, lanes in sides(backward(0, 2)):
        acc0[pl.ds(128, 384), lanes] += part

    chunk = 4 * BLOCK // head_count

    def out_copy(index, src, dst, j):
        to = lax.rem(h + j, head_count)
        n = dst.shape[0]
        return pltpu.make_async_remote_copy(
            src_ref=src.at[pl.ds(pl.multiple_of(to * n, n), n), :],
            dst_ref=dst.at[:, pl.ds(pl.multiple_of(h * BLOCK, BLOCK), BLOCK)],
            send_sem=out_send.at[index, to],
            recv_sem=out_recv.at[index, h],
            device_id={"head": to},
            device_id_type=MESH,
        )

    def out_arrival(index, dst, j):
        frm = lax.rem(h + j, head_count)
        here = dst.at[:, pl.ds(pl.multiple_of(frm * BLOCK, BLOCK), BLOCK)]
        pltpu.make_async_remote_copy(
            src_ref=here, dst_ref=here,
            send_sem=out_send.at[index, frm], recv_sem=out_recv.at[index, frm],
            device_id={"head": h}, device_id_type=MESH,
        ).wait_recv()

    def keep(src, dst):
        dst[:, pl.ds(pl.multiple_of(h * BLOCK, BLOCK), BLOCK)] = src[
            pl.ds(pl.multiple_of(h * dst.shape[0], dst.shape[0]), dst.shape[0]), :
        ]

    pl.semaphore_wait(core_sem, 1)
    for b in range(4):
        total = dq[pl.ds(OFF[4] + 8 * b, 8), :]
        for l in (3, 2, 1, 0):
            total = dq[pl.ds(OFF[l] + (BLOCK >> l) * b, BLOCK >> l), :] + 0.5 * expand(total, 1)
        oq[pl.ds(BLOCK * b, BLOCK), :] = dot(unperm, total.astype(BF16)).astype(BF16)
    for j in FAR_FIRST:
        out_copy(0, oq, gq_ref, j).start()
    keep(oq, gq_ref)

    for entry in at_level(4) + at_level(3):
        when(entry[4], lambda: back_arrival(entry))
    sum4 = rx4[pl.ds(0, BLOCK), :].astype(F32) + rx4[pl.ds(BLOCK, BLOCK), :].astype(F32)
    panel[...] = 0.5 * expand(sum4, 1)
    near_rows = pl.ds(pl.multiple_of(right * BLOCK, BLOCK), BLOCK)
    far_rows = pl.ds(pl.multiple_of((1 - right) * BLOCK, BLOCK), BLOCK)
    panel[near_rows, :] += rx3[pl.ds(0, BLOCK), :].astype(F32) + rx3[pl.ds(BLOCK, BLOCK), :].astype(F32)
    panel[far_rows, :] += rx3[pl.ds(2 * BLOCK, BLOCK), :].astype(F32)
    cots[...] = panel[...].astype(BF16)
    for d in (2, 1, 3):
        piece_back(d).start()

    for entry in at_level(1) + at_level(0):
        when(entry[4], lambda: back_arrival(entry))
    for b in range(4):
        sum1 = jnp.zeros((64, WIDE), F32)
        if b > 0:
            sum1 = sum1 + rx1[pl.ds(64 * (3 - b), 64), :].astype(F32)
        if b < 3:
            sum1 = sum1 + rx1[pl.ds(192 + 64 * (2 - b), 64), :].astype(F32)
        total = acc0[pl.ds(BLOCK * b, BLOCK), :] + 0.5 * expand(sum1, 1)
        if b == 0:
            total = total + rx0[pl.ds(0, BLOCK), :].astype(F32)
        if b == 3:
            total = total + rx0[pl.ds(BLOCK, BLOCK), :].astype(F32)
        done = dot(unperm, total.astype(BF16)).astype(BF16)
        ok[pl.ds(BLOCK * b, BLOCK), :] = done[:, :BLOCK]
        ov[pl.ds(BLOCK * b, BLOCK), :] = done[:, BLOCK:]
    for j in FAR_FIRST:
        out_copy(1, ok, gk_ref, j).start()
        out_copy(2, ov, gv_ref, j).start()
    keep(ok, gk_ref)
    keep(ov, gv_ref)

    for entry in at_level(2):
        when(entry[4], lambda: back_arrival(entry))
    sum3 = panel[pl.ds(pl.multiple_of(x * 64, 64), 64), :]
    for d in (1, 2, 3):
        row_arrival(parts, back_send, back_recv, d)
        frm = lax.rem(x + d, 4)
        sum3 = sum3 + parts[pl.ds(pl.multiple_of(frm * 64, 64), 64), :].astype(F32)
    sum2 = sum(rx2[pl.ds(128 * i, 128), :].astype(F32) for i in range(3)) + 0.5 * expand(sum3, 1)
    r64, c64 = row[:64, :64], col[:64, :64]
    nth = 8 * (r64 >> 4) + (r64 & 7)
    pick = jnp.where(
        c64 == 32 * ((r64 >> 3) & 1) + 8 * (nth & 3) + (nth >> 2), 1.0, 0.0
    ).astype(BF16)
    for b in range(4):
        part = sum2[32 * b : 32 * b + 32]
        part = jnp.concatenate([part[:, :BLOCK], part[:, BLOCK:]], axis=0).astype(BF16)
        oc[pl.ds(64 * b, 64), :] = dot(pick, part).astype(BF16)
    for j in FAR_FIRST:
        out_copy(3, oc, coarse, j).start()
    keep(oc, coarse)
    for entry in peers:
        when(entry[6], lambda: back_copy(entry).wait_send())
    for entry in outward:
        when(entry[4], lambda: forward_copy(entry).wait_send())
    for d in (1, 2, 3):
        piece_back(d).wait_send()
    for index, src, dst in ((0, oq, gq_ref), (1, ok, gk_ref), (2, ov, gv_ref), (3, oc, coarse)):
        for j in range(1, head_count):
            out_copy(index, src, dst, j).wait_send()
            out_arrival(index, dst, j)
    r16, c16 = row[:64, :16], col[:64, :16]
    spread = jnp.where(c16 == 8 * (r16 >> 5) + ((r16 & 31) >> 2), 0.25, 0.0).astype(BF16)
    more = dot(spread, coarse[...])
    gk_ref[...] = (gk_ref[...].astype(F32) + more[:chunk]).astype(BF16)
    gv_ref[...] = (gv_ref[...].astype(F32) + more[chunk:]).astype(BF16)


def write_out(a, b, c, d, a_out, b_out, c_out, d_out, sem):
    copies = [
        pltpu.make_async_copy(src, dst, sem.at[i])
        for i, (src, dst) in enumerate(((a, a_out), (b, b_out), (c, c_out), (d, d_out)))
    ]
    for copy in copies:
        copy.start()
    for copy in copies:
        copy.wait()


def solution(mesh):
    seq_count, head_count = mesh.shape["seq"], mesh.shape["head"]

    def step(queries, keys, values, grad_out):
        rows, width = queries.shape
        vmem = pl.BlockSpec(memory_space=pltpu.VMEM)
        grad = jax.ShapeDtypeStruct((rows // head_count, width * head_count), BF16)

        def wide(n, dtype=BF16):
            return pltpu.VMEM((n, WIDE), dtype)

        def stacked(dtype, width=BLOCK):
            return pltpu.VMEM((STACK, width), dtype)

        sems = pltpu.SemaphoreType.DMA
        results = pl.pallas_call(
            functools.partial(kernel, seq_count, head_count),
            out_shape=(jax.ShapeDtypeStruct((rows, width), BF16), grad, grad, grad),
            in_specs=[pl.BlockSpec(memory_space=pltpu.HBM)] * 4,
            out_specs=(vmem,) * 4,
            scratch_shapes=[
                wide(768), wide(256), wide(128), wide(64), wide(32),
                wide(512), wide(384), wide(384), wide(256),
                stacked(BF16), pltpu.VMEM((rows, width), F32), stacked(BF16, 384),
                stacked(F32), stacked(F32), stacked(F32), stacked(F32), stacked(F32), stacked(F32),
                wide(512, F32), wide(384, F32), wide(128, F32),
                wide(256), wide(512), wide(384), wide(384), wide(256),
                wide(256), wide(384), wide(384), wide(384), wide(256),
                wide(256, F32), wide(256), wide(256),
                *[pltpu.VMEM((rows, width), BF16) for _ in range(3)],
                pltpu.VMEM((256, BLOCK), BF16), pltpu.VMEM((16, width * head_count), BF16),
                *[pltpu.VMEM((rows, width), BF16) for _ in range(4)],
                sems((4,)),
                sems((OUT_SLOTS,)), sems((OUT_SLOTS,)), sems((SLOTS,)), sems((SLOTS,)),
                sems((4, head_count)), sems((4, head_count)),
                *[pltpu.SemaphoreType.REGULAR for _ in range(3)],
            ],
            compiler_params=pltpu.CompilerParams(
                collective_id=0, has_side_effects=True, vmem_limit_bytes=56000000
            ),
        )(queries, keys, values, grad_out)
        return pl.pallas_call(
            write_out,
            out_shape=tuple(jax.ShapeDtypeStruct(r.shape, r.dtype) for r in results),
            in_specs=[vmem] * 4,
            out_specs=(pl.BlockSpec(memory_space=pltpu.HBM),) * 4,
            scratch_shapes=[sems((4,))],
            compiler_params=pltpu.CompilerParams(vmem_limit_bytes=1024 * 1024),
        )(*results)

    return jax.shard_map(
        step,
        mesh=mesh,
        in_specs=(P("seq", "head"),) * 4,
        out_specs=(P("seq", "head"),) + (P(("seq", "head"), None),) * 3,
        check_vma=False,
    )
```

```python
import functools

import jax
import jax.numpy as jnp
from jax import lax
from jax.experimental import pallas as pl
from jax.experimental.pallas import tpu as pltpu
from jax.sharding import PartitionSpec as P

BLOCK = 128
WIDE = 256
NEG = -1e30
F32 = jnp.float32
BF16 = jnp.bfloat16
LOG2E = 1.4426950408889634
MESH = pl.DeviceIdType.MESH
OUT_SEM = (0, 2, 4, 7, 13)
OUT_SLOTS = 21
OUT_ROWS = (128, 192, 128, 64, 32)
OFF = (0, 512, 768, 896, 960)
STACK = 992
SEM = (0, 2, 4, 7, 10)
ROW_SEM = 12
SLOTS = 16
ROWS = (128, 192, 128, 128, 128)

SEND_ORDER = (0, 1, 4, 3, 2)
FIRST_FAR = 4
FAR_FIRST = (8, 7, 9, 6, 10, 5, 11, 4, 12, 3, 13, 2, 14, 1, 15)
NN = (((1,), (0,)), ((), ()))
NT = (((1,), (1,)), ((), ()))
TN = (((0,), (0,)), ((), ()))


def dot(a, b, dims=NN):
    return lax.dot_general(a, b, dims, preferred_element_type=F32)


def halve(x):
    n, w = x.shape
    x = x.reshape(n // 16, 2, 8, w)
    m = (x[:, 0] + x[:, 1]) * 0.5
    return m.astype(BF16).astype(F32).reshape(n // 2, w)


def expand(x, level):
    n, w = x.shape
    if level == 0:
        return x
    x = x.reshape(n // 8, 1, 8, w)
    x = jnp.broadcast_to(x, (n // 8, 1 << level, 8, w))
    return x.reshape(n << level, w)


def group(x, level):
    n, w = x.shape
    if level == 0:
        return x
    return x.reshape(n >> (level + 3), 1 << level, 8, w).sum(axis=1).reshape(n >> level, w)


def peers_of(s, seq_count):
    out = []

    def both(level, peer, slot, there, ok):
        out.append((level, peer, slot, there, ok, peer, ok))

    y, x = lax.div(s, 4), lax.rem(s, 4)
    up, down = lax.rem(s + seq_count - 4, seq_count), lax.rem(s + 4, seq_count)
    up_ok, down_ok = y > 0, y < 3
    right = x >= 2
    both(4, lax.rem(s + 8, seq_count), 0, 0, None)
    both(4, (3 - y) * 4 + x, 1, 1, (y == 0) | (y == 3))
    both(3, up, 0, 1, up_ok)
    both(3, down, 1, 0, down_ok)
    out.append((
        3, jnp.where(right, down, up), 2, 2,
        (right & down_ok) | (jnp.logical_not(right) & up_ok),
        jnp.where(right, up, down), (right & up_ok) | (jnp.logical_not(right) & down_ok),
    ))
    turn = 3 - 6 * lax.rem(s, 2)
    far = lax.rem(s + seq_count + turn, seq_count)
    both(2, far, 2, 2, (s + turn >= 0) & (s + turn < seq_count))
    both(2, lax.rem(s + seq_count - 2, seq_count), 0, 1, s >= 2)
    both(2, lax.rem(s + 2, seq_count), 1, 0, s + 2 < seq_count)
    prev, after = lax.rem(s + seq_count - 1, seq_count), lax.rem(s + 1, seq_count)
    for level in (1, 0):
        both(level, prev, 0, 1, s > 0)
        both(level, after, 1, 0, s + 1 < seq_count)
    return out


def direct_of(s, seq_count):
    out = []

    def both(level, peer, slot, there, ok):
        out.append((level, peer, slot, there, ok, peer, ok))

    a, e = lax.div(s, 2), lax.rem(s, 2)
    y, x = lax.div(s, 4), lax.rem(s, 4)
    blocks = seq_count // 2
    for f in range(4):
        both(4, lax.rem(y + 2, 4) * 4 + f, f, x, None)
    for f in range(4):
        both(4, (3 - y) * 4 + f, 4 + f, 4 + x, (y == 0) | (y == 3))
    turn = 3 - 6 * lax.rem(a, 2)
    far = lax.rem(a + blocks + turn, blocks)
    for f in range(2):
        both(3, far * 2 + f, 4 + f, 4 + e, (a + turn >= 0) & (a + turn < blocks))
    for f in range(2):
        both(3, lax.rem(a + blocks - 2, blocks) * 2 + f, f, 2 + e, a >= 2)
        both(3, lax.rem(a + 2, blocks) * 2 + f, 2 + f, e, a + 2 < blocks)
    return out


def when(ok, act):
    if ok is None:
        act()
    else:
        pl.when(ok)(act)


def kernel(
    seq_count, head_count,
    q_hbm, k_hbm, v_hbm, g_hbm,
    att_ref, gq_ref, gk_ref, gv_ref, coarse,
    kv0, kv1, kv2, kv3, kv4, in1, in2, in3, in4,
    qs, go, ee, pk, tot, sm, gg, dd, dq,
    acc0, acc1, edge, bk0, bk1, bk2, bk3, bk4, rx0, rx1, rx2, rx3, rx4,
    panel, cots, parts, oq, ok, ov, oc, q_ref, k_ref, v_ref, g_ref, load_sem,
    send_sem, recv_sem, back_send, back_recv, out_send, out_recv, row_sem, chip_sem, core_sem,
):
    s, h = lax.axis_index("seq"), lax.axis_index("head")
    barrier = pltpu.get_barrier_semaphore()
    loads = [
        pltpu.make_async_copy(src, dst, load_sem.at[i])
        for i, (src, dst) in enumerate(
            ((k_hbm, k_ref), (v_hbm, v_ref), (q_hbm, q_ref), (g_hbm, g_ref))
        )
    ]
    for load in loads:
        load.start()
    y, x = lax.div(s, 4), lax.rem(s, 4)
    row_mates = [y * 4 + lax.rem(x + d, 4) for d in (1, 2, 3)]
    near = [lax.rem(s + seq_count + d, seq_count) for d in (-1, 1)] + row_mates
    near += [lax.rem(s + 4 * d, seq_count) for d in (1, 2, 3)]
    core = h + 1 - 2 * lax.rem(h, 2)
    two_away = [lax.rem(h + d, head_count) for d in (4, head_count - 4)]
    near_head = [core] + two_away + [lax.rem(h + d, head_count) for d in (2, head_count - 2)]

    def tell(sem, axis, peers):
        for peer in peers:
            pl.semaphore_signal(sem, inc=1, device_id={axis: peer}, device_id_type=MESH)

    tell(barrier, "seq", near)
    tell(barrier, "head", near_head)

    row = lax.broadcasted_iota(jnp.int32, (BLOCK, BLOCK), 0)
    col = lax.broadcasted_iota(jnp.int32, (BLOCK, BLOCK), 1)
    perm = jnp.where(col == (row & 7) * 16 + (row >> 3), 1.0, 0.0).astype(BF16)
    unperm = jnp.where(col == (row & 15) * 8 + (row >> 4), 1.0, 0.0).astype(BF16)

    loads[0].wait()
    loads[1].wait()
    tops = []
    for b in range(4):
        rows = pl.ds(BLOCK * b, BLOCK)
        fine = dot(perm, jnp.concatenate([k_ref[rows, :], v_ref[rows, :]], axis=1))
        kv0[pl.ds(BLOCK + BLOCK * b, BLOCK), :] = fine.astype(BF16)
        m1 = halve(fine)
        kv1[pl.ds(64 * (3 - b), 64), :] = m1.astype(BF16)
        m2 = halve(m1)
        kv2[pl.ds(32 * b, 32), :] = m2.astype(BF16)
        m3 = halve(m2)
        kv3[pl.ds(16 * b, 16), :] = m3.astype(BF16)
        tops.append(halve(m3))
    kv4[...] = jnp.concatenate(tops, axis=0).astype(BF16)

    pl.semaphore_wait(barrier, len(near) + len(near_head))
    tell(row_sem, "seq", row_mates)
    tell(chip_sem, "head", two_away)

    peers = peers_of(s, seq_count)
    outward = [entry for entry in peers if entry[0] < 3] + direct_of(s, seq_count)
    inbox = (kv0, in1, in2, in3, in4)
    outbox = (bk0, bk1, bk2, bk3, bk4)
    rxbox = (rx0, rx1, rx2, rx3, rx4)

    right = lax.div(x, 2)

    def at_slot(ref, level, slot):
        n = ROWS[level]
        return ref.at[pl.ds(n * slot, n), :]

    def in_slot(level, slot):
        if level == 0:
            return kv0.at[pl.ds(640 * slot, BLOCK), :]
        if level == 1:
            return in1.at[pl.ds(64 + 192 * slot, 192), :]
        n = OUT_ROWS[level]
        return inbox[level].at[pl.ds(n * slot, n), :]

    def out_slot(level, slot):
        if level == 0:
            return kv0.at[pl.ds(BLOCK + 384 * slot, BLOCK), :]
        if level == 1:
            return kv1.at[pl.ds(64 * slot, 192), :]
        return (kv2, kv3, kv4)[level - 2]

    def forward_copy(entry):
        level, peer, slot, there = entry[:4]
        return pltpu.make_async_remote_copy(
            src_ref=out_slot(level, slot),
            dst_ref=in_slot(level, there),
            send_sem=send_sem.at[OUT_SEM[level] + slot],
            recv_sem=recv_sem.at[OUT_SEM[level] + there],
            device_id={"seq": peer},
            device_id_type=MESH,
        )

    def forward_arrival(entry):
        level, peer, slot = entry[:3]
        here = in_slot(level, slot)
        pltpu.make_async_remote_copy(
            src_ref=here, dst_ref=here,
            send_sem=send_sem.at[OUT_SEM[level] + slot], recv_sem=recv_sem.at[OUT_SEM[level] + slot],
            device_id={"seq": peer}, device_id_type=MESH,
        ).wait_recv()

    def back_slot(level, slot):
        if level == 1:
            return bk1.at[pl.ds(64 + 192 * slot, 192), :]
        return at_slot(outbox[level], level, slot)

    def back_copy(entry):
        level, _, slot, there, _, peer, _ = entry
        return pltpu.make_async_remote_copy(
            src_ref=back_slot(level, slot),
            dst_ref=at_slot(rxbox[level], level, there),
            send_sem=back_send.at[SEM[level] + slot],
            recv_sem=back_recv.at[SEM[level] + there],
            device_id={"seq": peer},
            device_id_type=MESH,
        )

    def back_arrival(entry):
        level, peer, slot = entry[:3]
        here = at_slot(rxbox[level], level, slot)
        pltpu.make_async_remote_copy(
            src_ref=here, dst_ref=here,
            send_sem=back_send.at[SEM[level] + slot], recv_sem=back_recv.at[SEM[level] + slot],
            device_id={"seq": peer}, device_id_type=MESH,
        ).wait_recv()

    def at_level(level):
        return [entry for entry in peers if entry[0] == level]

    def row_copy(src, dst, sends, recvs, d):
        to = lax.rem(x + d, 4)
        return pltpu.make_async_remote_copy(
            src_ref=src(to),
            dst_ref=dst.at[pl.ds(pl.multiple_of(x * 64, 64), 64), :],
            send_sem=sends.at[ROW_SEM + to],
            recv_sem=recvs.at[ROW_SEM + x],
            device_id={"seq": y * 4 + to},
            device_id_type=MESH,
        )

    def row_arrival(dst, sends, recvs, d):
        frm = lax.rem(x + d, 4)
        here = dst.at[pl.ds(pl.multiple_of(frm * 64, 64), 64), :]
        pltpu.make_async_remote_copy(
            src_ref=here, dst_ref=here,
            send_sem=sends.at[ROW_SEM + frm], recv_sem=recvs.at[ROW_SEM + frm],
            device_id={"seq": y * 4 + frm}, device_id_type=MESH,
        ).wait_recv()

    def piece_back(d):
        return row_copy(
            lambda to: cots.at[pl.ds(pl.multiple_of(to * 64, 64), 64), :],
            parts, back_send, back_recv, d,
        )

    def out_level(level):
        return [entry for entry in outward if entry[0] == level]

    for level in SEND_ORDER:
        if level == FIRST_FAR:
            pl.semaphore_wait(row_sem, len(row_mates))
        for entry in out_level(level):
            when(entry[4], lambda: forward_copy(entry).start())

    def clear(ref):
        ref[...] = jnp.zeros(ref.shape, BF16)

    for entry in outward:
        if entry[6] is not None:
            when(jnp.logical_not(entry[6]), lambda: clear(in_slot(entry[0], entry[2])))
    for entry in peers:
        if entry[4] is not None:
            when(
                jnp.logical_not(entry[4]),
                lambda: clear(at_slot(rxbox[entry[0]], entry[0], entry[2])),
            )

    loads[2].wait()
    loads[3].wait()
    tops = []
    for b in range(4):
        rows = pl.ds(BLOCK * b, BLOCK)
        both = dot(perm, jnp.concatenate([q_ref[rows, :], g_ref[rows, :]], axis=1))
        go[rows, :] = both[:, BLOCK:]
        fine = both[:, :BLOCK]
        qs[rows, :] = fine.astype(BF16)
        m1 = halve(fine)
        qs[pl.ds(OFF[1] + 64 * b, 64), :] = m1.astype(BF16)
        m2 = halve(m1)
        qs[pl.ds(OFF[2] + 32 * b, 32), :] = m2.astype(BF16)
        m3 = halve(m2)
        qs[pl.ds(OFF[3] + 16 * b, 16), :] = m3.astype(BF16)
        tops.append(halve(m3))
    qs[pl.ds(OFF[4], 32), :] = jnp.concatenate(tops, axis=0).astype(BF16)

    scale = BLOCK ** (-0.5)
    lane = lax.broadcasted_iota(jnp.int32, (8, 384), 1)

    def off_if(bad):
        return jnp.where(bad, NEG, 0.0).astype(F32)

    no_prev, no_next = off_if(s == 0), off_if(s == seq_count - 1)
    a = lax.div(s, 2)

    def thirds(first, second, last):
        return jnp.where(lane < 128, first, jnp.where(lane < 256, second, last))[:1]

    def slot_bias(i, n):
        even = lax.rem(i, 2) == 0
        return thirds(
            off_if(i < 2), off_if(i + 2 > n - 1),
            off_if((even & (i + 3 > n - 1)) | (jnp.logical_not(even) & (i < 3))),
        )

    bias1 = (
        thirds(no_prev, no_next, no_next),
        thirds(no_prev, no_prev, no_next),
    )
    bias2 = slot_bias(s, seq_count)
    bias3 = slot_bias(a, seq_count // 2)
    bias4 = thirds(jnp.zeros((), F32), off_if((y == 1) | (y == 2)), jnp.zeros((), F32))[:, :256]

    def unit(level, c):
        if level == 0:
            bias = {0: thirds(no_prev, 0.0, 0.0), 3: thirds(0.0, 0.0, no_next)}.get(c)
            return (OFF[0] + BLOCK * c, BLOCK, kv0, BLOCK * c, 384, bias)
        if level == 1:
            return (OFF[1] + BLOCK * c, BLOCK, in1, BLOCK * (1 - c), 384, bias1[c])
        if level == 2:
            return (OFF[2], 128, in2, 0, 384, bias2)
        if level == 3:
            return (OFF[3], 64, in3, 0, 384, bias3)
        return (OFF[4], 32, in4, 0, 256, bias4)

    def forward(level, c=0):
        r0, n, ref, k0, m, bias = unit(level, c)
        rows, keys = pl.ds(r0, n), pl.ds(k0, m)
        sc = dot(qs[rows, :], ref[keys, :BLOCK], NT) * (scale * LOG2E)
        if bias is not None:
            sc = sc + bias
        top = jnp.max(sc, axis=1, keepdims=True)
        e = jnp.exp2(sc - top)
        pk[rows, :] = jnp.broadcast_to(top, (n, BLOCK))
        tot[rows, :] = jnp.broadcast_to(jnp.sum(e, axis=1, keepdims=True), (n, BLOCK))
        eb = e.astype(BF16)
        ee[rows, :m] = eb
        sm[rows, :] = dot(eb, ref[keys, BLOCK:])

    forward(0, 1)
    forward(0, 2)
    for level in SEND_ORDER:
        for entry in out_level(level):
            when(entry[6], lambda: forward_arrival(entry))
        if level == 0:
            in1[pl.ds(0, 64), :] = halve(kv0[pl.ds(0, BLOCK), :].astype(F32)).astype(BF16)
            in1[pl.ds(448, 64), :] = halve(kv0[pl.ds(640, BLOCK), :].astype(F32)).astype(BF16)
            forward(0, 0)
            forward(0, 3)
        elif level == 1:
            forward(1, 0)
            forward(1, 1)
        else:
            forward(level)

    pl.semaphore_wait(chip_sem, len(two_away))
    tell(core_sem, "head", [core])

    for b in range(4):
        where = [pl.ds(OFF[l] + (BLOCK >> l) * b, BLOCK >> l) for l in range(5)]
        peaks = [expand(pk[where[l], :], l) for l in range(5)]
        overall = functools.reduce(jnp.maximum, peaks)
        factors = [jnp.exp2(peaks[l] - overall) * float(1 << l) for l in range(5)]
        den = sum(factors[l] * expand(tot[where[l], :], l) for l in range(5))
        num = sum(factors[l] * expand(sm[where[l], :], l) for l in range(5))
        inverse = 1.0 / den
        out = num * inverse
        att_ref[pl.ds(BLOCK * b, BLOCK), :] = dot(unperm, out.astype(BF16)).astype(BF16)
        cot = go[pl.ds(BLOCK * b, BLOCK), :]
        delta = jnp.broadcast_to(jnp.sum(cot * out, axis=1, keepdims=True), (BLOCK, BLOCK))
        cot, delta = cot * inverse, delta * inverse
        for l in range(5):
            gg[where[l], :] = group(factors[l] * cot, l)
            dd[where[l], :] = group(factors[l] * delta, l)

    def backward(level, c=0):
        r0, n, ref, k0, m, _ = unit(level, c)
        rows, keys = pl.ds(r0, n), pl.ds(k0, m)
        gb = gg[rows, :].astype(BF16)
        eb = ee[rows, :m]
        shift = jnp.concatenate([dd[rows, :]] * (m // BLOCK), axis=1)
        ds = eb.astype(F32) * (dot(gb, ref[keys, BLOCK:], NT) - shift)
        ds = (ds * scale).astype(BF16)
        dq[rows, :] = dot(ds, ref[keys, :BLOCK])
        return dot(ds, qs[rows, :], TN), dot(eb, gb, TN)

    def sides(parts):
        return ((parts[0], pl.ds(0, BLOCK)), (parts[1], pl.ds(BLOCK, BLOCK)))

    def start_back(level):
        for entry in peers:
            if entry[0] == level:
                when(entry[6], lambda: back_copy(entry).start())

    for level in (4, 3):
        for part, lanes in sides(backward(level)):
            outbox[level][:, lanes] = part.astype(BF16)
        start_back(level)
    for part, lanes in sides(backward(1, 0)):
        acc1[pl.ds(0, 384), lanes] = part
    for part, lanes in sides(backward(1, 1)):
        edge[pl.ds(0, 64), lanes] = part[:64]
        bk1[pl.ds(64, 64), lanes] = part[64:128].astype(BF16)
        bk1[pl.ds(128, 256), lanes] = (part[128:] + acc1[pl.ds(0, 256), lanes]).astype(BF16)
        bk1[pl.ds(384, 64), lanes] = acc1[pl.ds(256, 64), lanes].astype(BF16)
        edge[pl.ds(64, 64), lanes] = acc1[pl.ds(320, 64), lanes]
    start_back(1)
    for part, lanes in sides(backward(0, 0)):
        fold = 0.5 * expand(edge[pl.ds(0, 64), lanes], 1)
        bk0[pl.ds(0, 128), lanes] = (part[:128] + fold).astype(BF16)
        acc0[pl.ds(0, 256), lanes] = part[128:]
    for part, lanes in sides(backward(0, 3)):
        acc0[pl.ds(256, 256), lanes] = part[:256]
        fold = 0.5 * expand(edge[pl.ds(64, 64), lanes], 1)
        bk0[pl.ds(128, 128), lanes] = (part[256:] + fold).astype(BF16)
    start_back(0)
    for level in (2,):
        for part, lanes in sides(backward(level)):
            outbox[level][:, lanes] = part.astype(BF16)
        start_back(level)
    for part, lanes in sides(backward(0, 1)):
        acc0[pl.ds(0, 384), lanes] += part
    for part, lanes in sides(backward(0, 2)):
        acc0[pl.ds(128, 384), lanes] += part

    chunk = 4 * BLOCK // head_count

    def out_copy(index, src, dst, j):
        to = lax.rem(h + j, head_count)
        n = dst.shape[0]
        return pltpu.make_async_remote_copy(
            src_ref=src.at[pl.ds(pl.multiple_of(to * n, n), n), :],
            dst_ref=dst.at[:, pl.ds(pl.multiple_of(h * BLOCK, BLOCK), BLOCK)],
            send_sem=out_send.at[index, to],
            recv_sem=out_recv.at[index, h],
            device_id={"head": to},
            device_id_type=MESH,
        )

    def out_arrival(index, dst, j):
        frm = lax.rem(h + j, head_count)
        here = dst.at[:, pl.ds(pl.multiple_of(frm * BLOCK, BLOCK), BLOCK)]
        pltpu.make_async_remote_copy(
            src_ref=here, dst_ref=here,
            send_sem=out_send.at[index, frm], recv_sem=out_recv.at[index, frm],
            device_id={"head": h}, device_id_type=MESH,
        ).wait_recv()

    def keep(src, dst):
        dst[:, pl.ds(pl.multiple_of(h * BLOCK, BLOCK), BLOCK)] = src[
            pl.ds(pl.multiple_of(h * dst.shape[0], dst.shape[0]), dst.shape[0]), :
        ]

    pl.semaphore_wait(core_sem, 1)
    for b in range(4):
        total = dq[pl.ds(OFF[4] + 8 * b, 8), :]
        for l in (3, 2, 1, 0):
            total = dq[pl.ds(OFF[l] + (BLOCK >> l) * b, BLOCK >> l), :] + 0.5 * expand(total, 1)
        oq[pl.ds(BLOCK * b, BLOCK), :] = dot(unperm, total.astype(BF16)).astype(BF16)
    for j in FAR_FIRST:
        out_copy(0, oq, gq_ref, j).start()
    keep(oq, gq_ref)

    for entry in at_level(4) + at_level(3):
        when(entry[4], lambda: back_arrival(entry))
    sum4 = rx4[pl.ds(0, BLOCK), :].astype(F32) + rx4[pl.ds(BLOCK, BLOCK), :].astype(F32)
    panel[...] = 0.5 * expand(sum4, 1)
    near_rows = pl.ds(pl.multiple_of(right * BLOCK, BLOCK), BLOCK)
    far_rows = pl.ds(pl.multiple_of((1 - right) * BLOCK, BLOCK), BLOCK)
    panel[near_rows, :] += rx3[pl.ds(0, BLOCK), :].astype(F32) + rx3[pl.ds(BLOCK, BLOCK), :].astype(F32)
    panel[far_rows, :] += rx3[pl.ds(2 * BLOCK, BLOCK), :].astype(F32)
    cots[...] = panel[...].astype(BF16)
    for d in (2, 1, 3):
        piece_back(d).start()

    for entry in at_level(1) + at_level(0):
        when(entry[4], lambda: back_arrival(entry))
    for b in range(4):
        sum1 = jnp.zeros((64, WIDE), F32)
        if b > 0:
            sum1 = sum1 + rx1[pl.ds(64 * (3 - b), 64), :].astype(F32)
        if b < 3:
            sum1 = sum1 + rx1[pl.ds(192 + 64 * (2 - b), 64), :].astype(F32)
        total = acc0[pl.ds(BLOCK * b, BLOCK), :] + 0.5 * expand(sum1, 1)
        if b == 0:
            total = total + rx0[pl.ds(0, BLOCK), :].astype(F32)
        if b == 3:
            total = total + rx0[pl.ds(BLOCK, BLOCK), :].astype(F32)
        done = dot(unperm, total.astype(BF16)).astype(BF16)
        ok[pl.ds(BLOCK * b, BLOCK), :] = done[:, :BLOCK]
        ov[pl.ds(BLOCK * b, BLOCK), :] = done[:, BLOCK:]
    for j in FAR_FIRST:
        out_copy(1, ok, gk_ref, j).start()
        out_copy(2, ov, gv_ref, j).start()
    keep(ok, gk_ref)
    keep(ov, gv_ref)

    for entry in at_level(2):
        when(entry[4], lambda: back_arrival(entry))
    sum3 = panel[pl.ds(pl.multiple_of(x * 64, 64), 64), :]
    for d in (1, 2, 3):
        row_arrival(parts, back_send, back_recv, d)
        frm = lax.rem(x + d, 4)
        sum3 = sum3 + parts[pl.ds(pl.multiple_of(frm * 64, 64), 64), :].astype(F32)
    sum2 = sum(rx2[pl.ds(128 * i, 128), :].astype(F32) for i in range(3)) + 0.5 * expand(sum3, 1)
    r64, c64 = row[:64, :64], col[:64, :64]
    nth = 8 * (r64 >> 4) + (r64 & 7)
    pick = jnp.where(
        c64 == 32 * ((r64 >> 3) & 1) + 8 * (nth & 3) + (nth >> 2), 1.0, 0.0
    ).astype(BF16)
    for b in range(4):
        part = sum2[32 * b : 32 * b + 32]
        part = jnp.concatenate([part[:, :BLOCK], part[:, BLOCK:]], axis=0).astype(BF16)
        oc[pl.ds(64 * b, 64), :] = dot(pick, part).astype(BF16)
    for j in FAR_FIRST:
        out_copy(3, oc, coarse, j).start()
    keep(oc, coarse)
    for entry in peers:
        when(entry[6], lambda: back_copy(entry).wait_send())
    for entry in outward:
        when(entry[4], lambda: forward_copy(entry).wait_send())
    for d in (1, 2, 3):
        piece_back(d).wait_send()
    for index, src, dst in ((0, oq, gq_ref), (1, ok, gk_ref), (2, ov, gv_ref), (3, oc, coarse)):
        for j in range(1, head_count):
            out_copy(index, src, dst, j).wait_send()
            out_arrival(index, dst, j)


def write_out(a, b, c, d, coarse, a_out, b_out, c_out, d_out, keys, values, sem):
    copies = [
        pltpu.make_async_copy(src, dst, sem.at[i])
        for i, (src, dst) in enumerate(((a, a_out), (b, b_out), (keys, c_out), (values, d_out)))
    ]
    copies[0].start()
    copies[1].start()
    chunk = c.shape[0]
    r16 = lax.broadcasted_iota(jnp.int32, (2 * chunk, 16), 0)
    c16 = lax.broadcasted_iota(jnp.int32, (2 * chunk, 16), 1)
    spread = jnp.where(c16 == 8 * (r16 >> 5) + ((r16 & 31) >> 2), 0.25, 0.0).astype(BF16)
    more = dot(spread, coarse[...])
    keys[...] = (c[...].astype(F32) + more[:chunk]).astype(BF16)
    copies[2].start()
    values[...] = (d[...].astype(F32) + more[chunk:]).astype(BF16)
    copies[3].start()
    for copy in copies:
        copy.wait()


def solution(mesh):
    seq_count, head_count = mesh.shape["seq"], mesh.shape["head"]

    def step(queries, keys, values, grad_out):
        rows, width = queries.shape
        vmem = pl.BlockSpec(memory_space=pltpu.VMEM)
        grad = jax.ShapeDtypeStruct((rows // head_count, width * head_count), BF16)

        def wide(n, dtype=BF16):
            return pltpu.VMEM((n, WIDE), dtype)

        def stacked(dtype, width=BLOCK):
            return pltpu.VMEM((STACK, width), dtype)

        sems = pltpu.SemaphoreType.DMA
        results = pl.pallas_call(
            functools.partial(kernel, seq_count, head_count),
            out_shape=(
                jax.ShapeDtypeStruct((rows, width), BF16), grad, grad, grad,
                jax.ShapeDtypeStruct((16, width * head_count), BF16),
            ),
            in_specs=[pl.BlockSpec(memory_space=pltpu.HBM)] * 4,
            out_specs=(vmem,) * 5,
            scratch_shapes=[
                wide(768), wide(256), wide(128), wide(64), wide(32),
                wide(512), wide(384), wide(384), wide(256),
                stacked(BF16), pltpu.VMEM((rows, width), F32), stacked(BF16, 384),
                stacked(F32), stacked(F32), stacked(F32), stacked(F32), stacked(F32), stacked(F32),
                wide(512, F32), wide(384, F32), wide(128, F32),
                wide(256), wide(512), wide(384), wide(384), wide(256),
                wide(256), wide(384), wide(384), wide(384), wide(256),
                wide(256, F32), wide(256), wide(256),
                *[pltpu.VMEM((rows, width), BF16) for _ in range(3)],
                pltpu.VMEM((256, BLOCK), BF16),
                *[pltpu.VMEM((rows, width), BF16) for _ in range(4)],
                sems((4,)),
                sems((OUT_SLOTS,)), sems((OUT_SLOTS,)), sems((SLOTS,)), sems((SLOTS,)),
                sems((4, head_count)), sems((4, head_count)),
                *[pltpu.SemaphoreType.REGULAR for _ in range(3)],
            ],
            compiler_params=pltpu.CompilerParams(
                collective_id=0, has_side_effects=True, vmem_limit_bytes=55900000
            ),
        )(queries, keys, values, grad_out)
        return pl.pallas_call(
            write_out,
            out_shape=tuple(jax.ShapeDtypeStruct(r.shape, r.dtype) for r in results[:4]),
            in_specs=[vmem] * 5,
            out_specs=(pl.BlockSpec(memory_space=pltpu.HBM),) * 4,
            scratch_shapes=[pltpu.VMEM(grad.shape, BF16), pltpu.VMEM(grad.shape, BF16), sems((4,))],
            compiler_params=pltpu.CompilerParams(vmem_limit_bytes=1024 * 1024),
        )(*results)

    return jax.shard_map(
        step,
        mesh=mesh,
        in_specs=(P("seq", "head"),) * 4,
        out_specs=(P("seq", "head"),) + (P(("seq", "head"), None),) * 3,
        check_vma=False,
    )
```

```python
import functools

import jax
import jax.numpy as jnp
from jax import lax
from jax.experimental import pallas as pl
from jax.experimental.pallas import tpu as pltpu
from jax.sharding import PartitionSpec as P

BLOCK = 128
WIDE = 256
NEG = -1e30
F32 = jnp.float32
BF16 = jnp.bfloat16
LOG2E = 1.4426950408889634
MESH = pl.DeviceIdType.MESH
OUT_SEM = (0, 2, 4, 7, 13)
OUT_SLOTS = 21
OUT_ROWS = (128, 192, 128, 64, 32)
OFF = (0, 512, 768, 896, 960)
STACK = 992
SEM = (0, 2, 4, 7, 10)
ROW_SEM = 12
SLOTS = 16
ROWS = (128, 192, 128, 128, 128)

SEND_ORDER = (0, 1, 4, 3, 2)
FAR_FIRST = (8, 7, 9, 6, 10, 5, 11, 4, 12, 3, 13, 2, 14, 1, 15)
NN = (((1,), (0,)), ((), ()))
NT = (((1,), (1,)), ((), ()))
TN = (((0,), (0,)), ((), ()))


def dot(a, b, dims=NN):
    return lax.dot_general(a, b, dims, preferred_element_type=F32)


def halve(x):
    n, w = x.shape
    x = x.reshape(n // 16, 2, 8, w)
    m = (x[:, 0] + x[:, 1]) * 0.5
    return m.astype(BF16).astype(F32).reshape(n // 2, w)


def expand(x, level):
    n, w = x.shape
    if level == 0:
        return x
    x = x.reshape(n // 8, 1, 8, w)
    x = jnp.broadcast_to(x, (n // 8, 1 << level, 8, w))
    return x.reshape(n << level, w)


def group(x, level):
    n, w = x.shape
    if level == 0:
        return x
    return x.reshape(n >> (level + 3), 1 << level, 8, w).sum(axis=1).reshape(n >> level, w)


def peers_of(s, seq_count):
    out = []

    def both(level, peer, slot, there, ok):
        out.append((level, peer, slot, there, ok, peer, ok))

    y, x = lax.div(s, 4), lax.rem(s, 4)
    up, down = lax.rem(s + seq_count - 4, seq_count), lax.rem(s + 4, seq_count)
    up_ok, down_ok = y > 0, y < 3
    right = x >= 2
    both(4, lax.rem(s + 8, seq_count), 0, 0, None)
    both(4, (3 - y) * 4 + x, 1, 1, (y == 0) | (y == 3))
    both(3, up, 0, 1, up_ok)
    both(3, down, 1, 0, down_ok)
    out.append((
        3, jnp.where(right, down, up), 2, 2,
        (right & down_ok) | (jnp.logical_not(right) & up_ok),
        jnp.where(right, up, down), (right & up_ok) | (jnp.logical_not(right) & down_ok),
    ))
    turn = 3 - 6 * lax.rem(s, 2)
    far = lax.rem(s + seq_count + turn, seq_count)
    both(2, far, 2, 2, (s + turn >= 0) & (s + turn < seq_count))
    both(2, lax.rem(s + seq_count - 2, seq_count), 0, 1, s >= 2)
    both(2, lax.rem(s + 2, seq_count), 1, 0, s + 2 < seq_count)
    prev, after = lax.rem(s + seq_count - 1, seq_count), lax.rem(s + 1, seq_count)
    for level in (1, 0):
        both(level, prev, 0, 1, s > 0)
        both(level, after, 1, 0, s + 1 < seq_count)
    return out


def direct_of(s, seq_count):
    out = []

    def both(level, peer, slot, there, ok):
        out.append((level, peer, slot, there, ok, peer, ok))

    a, e = lax.div(s, 2), lax.rem(s, 2)
    y, x = lax.div(s, 4), lax.rem(s, 4)
    blocks = seq_count // 2
    for f in range(4):
        both(4, lax.rem(y + 2, 4) * 4 + f, f, x, None)
    for f in range(4):
        both(4, (3 - y) * 4 + f, 4 + f, 4 + x, (y == 0) | (y == 3))
    turn = 3 - 6 * lax.rem(a, 2)
    far = lax.rem(a + blocks + turn, blocks)
    for f in range(2):
        both(3, far * 2 + f, 4 + f, 4 + e, (a + turn >= 0) & (a + turn < blocks))
    for f in range(2):
        both(3, lax.rem(a + blocks - 2, blocks) * 2 + f, f, 2 + e, a >= 2)
        both(3, lax.rem(a + 2, blocks) * 2 + f, 2 + f, e, a + 2 < blocks)
    return out


def when(ok, act):
    if ok is None:
        act()
    else:
        pl.when(ok)(act)


def kernel(
    seq_count, head_count,
    q_hbm, k_hbm, v_hbm, g_hbm,
    att_ref, gq_ref, gk_ref, gv_ref,
    kv0, kv1, kv2, kv3, kv4, in1, in2, in3, in4,
    qs, go, ee, pk, tot, sm, gg, dd, dq,
    acc0, acc1, edge, bk0, bk1, bk2, bk3, bk4, rx0, rx1, rx2, rx3, rx4,
    panel, cots, parts, oa, oq, ok, ov, oc, coarse, q_ref, k_ref, v_ref, g_ref, load_sem,
    send_sem, recv_sem, back_send, back_recv, out_send, out_recv, row_sem, chip_sem, core_sem,
):
    s, h = lax.axis_index("seq"), lax.axis_index("head")
    barrier = pltpu.get_barrier_semaphore()
    loads = [
        pltpu.make_async_copy(src, dst, load_sem.at[i])
        for i, (src, dst) in enumerate(
            ((k_hbm, k_ref), (v_hbm, v_ref), (q_hbm, q_ref), (g_hbm, g_ref))
        )
    ]
    for load in loads:
        load.start()
    y, x = lax.div(s, 4), lax.rem(s, 4)
    row_mates = [y * 4 + lax.rem(x + d, 4) for d in (1, 2, 3)]
    near = [lax.rem(s + seq_count + d, seq_count) for d in (-1, 1)] + row_mates
    near += [lax.rem(s + 4 * d, seq_count) for d in (1, 2, 3)]
    core = h + 1 - 2 * lax.rem(h, 2)
    two_away = [lax.rem(h + d, head_count) for d in (4, head_count - 4)]
    near_head = [core] + two_away + [lax.rem(h + d, head_count) for d in (2, head_count - 2)]

    def tell(sem, axis, peers):
        for peer in peers:
            pl.semaphore_signal(sem, inc=1, device_id={axis: peer}, device_id_type=MESH)

    tell(barrier, "seq", near)
    tell(barrier, "head", near_head)

    row = lax.broadcasted_iota(jnp.int32, (BLOCK, BLOCK), 0)
    col = lax.broadcasted_iota(jnp.int32, (BLOCK, BLOCK), 1)
    perm = jnp.where(col == (row & 7) * 16 + (row >> 3), 1.0, 0.0).astype(BF16)
    unperm = jnp.where(col == (row & 15) * 8 + (row >> 4), 1.0, 0.0).astype(BF16)

    loads[0].wait()
    loads[1].wait()
    tops = []
    for b in range(4):
        rows = pl.ds(BLOCK * b, BLOCK)
        fine = dot(perm, jnp.concatenate([k_ref[rows, :], v_ref[rows, :]], axis=1))
        kv0[pl.ds(BLOCK + BLOCK * b, BLOCK), :] = fine.astype(BF16)
        m1 = halve(fine)
        kv1[pl.ds(64 * (3 - b), 64), :] = m1.astype(BF16)
        m2 = halve(m1)
        kv2[pl.ds(32 * b, 32), :] = m2.astype(BF16)
        m3 = halve(m2)
        kv3[pl.ds(16 * b, 16), :] = m3.astype(BF16)
        tops.append(halve(m3))
    kv4[...] = jnp.concatenate(tops, axis=0).astype(BF16)

    pl.semaphore_wait(barrier, len(near) + len(near_head))
    tell(row_sem, "seq", row_mates)
    tell(chip_sem, "head", two_away)

    peers = peers_of(s, seq_count)
    outward = [entry for entry in peers if entry[0] < 3] + direct_of(s, seq_count)
    inbox = (kv0, in1, in2, in3, in4)
    outbox = (bk0, bk1, bk2, bk3, bk4)
    rxbox = (rx0, rx1, rx2, rx3, rx4)

    right = lax.div(x, 2)

    def at_slot(ref, level, slot):
        n = ROWS[level]
        return ref.at[pl.ds(n * slot, n), :]

    def in_slot(level, slot):
        if level == 0:
            return kv0.at[pl.ds(640 * slot, BLOCK), :]
        if level == 1:
            return in1.at[pl.ds(64 + 192 * slot, 192), :]
        n = OUT_ROWS[level]
        return inbox[level].at[pl.ds(n * slot, n), :]

    def out_slot(level, slot):
        if level == 0:
            return kv0.at[pl.ds(BLOCK + 384 * slot, BLOCK), :]
        if level == 1:
            return kv1.at[pl.ds(64 * slot, 192), :]
        return (kv2, kv3, kv4)[level - 2]

    def forward_copy(entry):
        level, peer, slot, there = entry[:4]
        return pltpu.make_async_remote_copy(
            src_ref=out_slot(level, slot),
            dst_ref=in_slot(level, there),
            send_sem=send_sem.at[OUT_SEM[level] + slot],
            recv_sem=recv_sem.at[OUT_SEM[level] + there],
            device_id={"seq": peer},
            device_id_type=MESH,
        )

    def forward_arrival(entry):
        level, peer, slot = entry[:3]
        here = in_slot(level, slot)
        pltpu.make_async_remote_copy(
            src_ref=here, dst_ref=here,
            send_sem=send_sem.at[OUT_SEM[level] + slot], recv_sem=recv_sem.at[OUT_SEM[level] + slot],
            device_id={"seq": peer}, device_id_type=MESH,
        ).wait_recv()

    def back_slot(level, slot):
        if level == 1:
            return bk1.at[pl.ds(64 + 192 * slot, 192), :]
        return at_slot(outbox[level], level, slot)

    def back_copy(entry):
        level, _, slot, there, _, peer, _ = entry
        return pltpu.make_async_remote_copy(
            src_ref=back_slot(level, slot),
            dst_ref=at_slot(rxbox[level], level, there),
            send_sem=back_send.at[SEM[level] + slot],
            recv_sem=back_recv.at[SEM[level] + there],
            device_id={"seq": peer},
            device_id_type=MESH,
        )

    def back_arrival(entry):
        level, peer, slot = entry[:3]
        here = at_slot(rxbox[level], level, slot)
        pltpu.make_async_remote_copy(
            src_ref=here, dst_ref=here,
            send_sem=back_send.at[SEM[level] + slot], recv_sem=back_recv.at[SEM[level] + slot],
            device_id={"seq": peer}, device_id_type=MESH,
        ).wait_recv()

    def at_level(level):
        return [entry for entry in peers if entry[0] == level]

    def row_copy(src, dst, sends, recvs, d):
        to = lax.rem(x + d, 4)
        return pltpu.make_async_remote_copy(
            src_ref=src(to),
            dst_ref=dst.at[pl.ds(pl.multiple_of(x * 64, 64), 64), :],
            send_sem=sends.at[ROW_SEM + to],
            recv_sem=recvs.at[ROW_SEM + x],
            device_id={"seq": y * 4 + to},
            device_id_type=MESH,
        )

    def row_arrival(dst, sends, recvs, d):
        frm = lax.rem(x + d, 4)
        here = dst.at[pl.ds(pl.multiple_of(frm * 64, 64), 64), :]
        pltpu.make_async_remote_copy(
            src_ref=here, dst_ref=here,
            send_sem=sends.at[ROW_SEM + frm], recv_sem=recvs.at[ROW_SEM + frm],
            device_id={"seq": y * 4 + frm}, device_id_type=MESH,
        ).wait_recv()

    def piece_back(d):
        return row_copy(
            lambda to: cots.at[pl.ds(pl.multiple_of(to * 64, 64), 64), :],
            parts, back_send, back_recv, d,
        )

    def out_level(level):
        return [entry for entry in outward if entry[0] == level]

    for level in (0, 1):
        for entry in out_level(level):
            when(entry[4], lambda: forward_copy(entry).start())

    def clear(ref):
        ref[...] = jnp.zeros(ref.shape, BF16)

    for entry in outward:
        if entry[6] is not None:
            when(jnp.logical_not(entry[6]), lambda: clear(in_slot(entry[0], entry[2])))
    for entry in peers:
        if entry[4] is not None:
            when(
                jnp.logical_not(entry[4]),
                lambda: clear(at_slot(rxbox[entry[0]], entry[0], entry[2])),
            )

    loads[2].wait()
    loads[3].wait()
    tops = []
    for b in range(4):
        rows = pl.ds(BLOCK * b, BLOCK)
        both = dot(perm, jnp.concatenate([q_ref[rows, :], g_ref[rows, :]], axis=1))
        go[rows, :] = both[:, BLOCK:]
        fine = both[:, :BLOCK]
        qs[rows, :] = fine.astype(BF16)
        m1 = halve(fine)
        qs[pl.ds(OFF[1] + 64 * b, 64), :] = m1.astype(BF16)
        m2 = halve(m1)
        qs[pl.ds(OFF[2] + 32 * b, 32), :] = m2.astype(BF16)
        m3 = halve(m2)
        qs[pl.ds(OFF[3] + 16 * b, 16), :] = m3.astype(BF16)
        tops.append(halve(m3))
    qs[pl.ds(OFF[4], 32), :] = jnp.concatenate(tops, axis=0).astype(BF16)

    pl.semaphore_wait(row_sem, len(row_mates))
    for level in (4, 3, 2):
        for entry in out_level(level):
            when(entry[4], lambda: forward_copy(entry).start())

    scale = BLOCK ** (-0.5)
    lane = lax.broadcasted_iota(jnp.int32, (8, 384), 1)

    def off_if(bad):
        return jnp.where(bad, NEG, 0.0).astype(F32)

    no_prev, no_next = off_if(s == 0), off_if(s == seq_count - 1)
    a = lax.div(s, 2)

    def thirds(first, second, last):
        return jnp.where(lane < 128, first, jnp.where(lane < 256, second, last))[:1]

    def slot_bias(i, n):
        even = lax.rem(i, 2) == 0
        return thirds(
            off_if(i < 2), off_if(i + 2 > n - 1),
            off_if((even & (i + 3 > n - 1)) | (jnp.logical_not(even) & (i < 3))),
        )

    bias1 = (
        thirds(no_prev, no_next, no_next),
        thirds(no_prev, no_prev, no_next),
    )
    bias2 = slot_bias(s, seq_count)
    bias3 = slot_bias(a, seq_count // 2)
    bias4 = thirds(jnp.zeros((), F32), off_if((y == 1) | (y == 2)), jnp.zeros((), F32))[:, :256]

    def unit(level, c):
        if level == 0:
            bias = {0: thirds(no_prev, 0.0, 0.0), 3: thirds(0.0, 0.0, no_next)}.get(c)
            return (OFF[0] + BLOCK * c, BLOCK, kv0, BLOCK * c, 384, bias)
        if level == 1:
            return (OFF[1] + BLOCK * c, BLOCK, in1, BLOCK * (1 - c), 384, bias1[c])
        if level == 2:
            return (OFF[2], 128, in2, 0, 384, bias2)
        if level == 3:
            return (OFF[3], 64, in3, 0, 384, bias3)
        return (OFF[4], 32, in4, 0, 256, bias4)

    def forward(level, c=0):
        r0, n, ref, k0, m, bias = unit(level, c)
        rows, keys = pl.ds(r0, n), pl.ds(k0, m)
        sc = dot(qs[rows, :], ref[keys, :BLOCK], NT) * (scale * LOG2E)
        if bias is not None:
            sc = sc + bias
        top = jnp.max(sc, axis=1, keepdims=True)
        e = jnp.exp2(sc - top)
        pk[rows, :] = jnp.broadcast_to(top, (n, BLOCK))
        tot[rows, :] = jnp.broadcast_to(jnp.sum(e, axis=1, keepdims=True), (n, BLOCK))
        eb = e.astype(BF16)
        ee[rows, :m] = eb
        sm[rows, :] = dot(eb, ref[keys, BLOCK:])

    forward(0, 1)
    forward(0, 2)
    for level in SEND_ORDER:
        for entry in out_level(level):
            when(entry[6], lambda: forward_arrival(entry))
        if level == 0:
            in1[pl.ds(0, 64), :] = halve(kv0[pl.ds(0, BLOCK), :].astype(F32)).astype(BF16)
            in1[pl.ds(448, 64), :] = halve(kv0[pl.ds(640, BLOCK), :].astype(F32)).astype(BF16)
            forward(0, 0)
            forward(0, 3)
        elif level == 1:
            forward(1, 0)
            forward(1, 1)
        else:
            forward(level)

    pl.semaphore_wait(chip_sem, len(two_away))
    tell(core_sem, "head", [core])

    for b in range(4):
        where = [pl.ds(OFF[l] + (BLOCK >> l) * b, BLOCK >> l) for l in range(5)]
        peaks = [expand(pk[where[l], :], l) for l in range(5)]
        overall = functools.reduce(jnp.maximum, peaks)
        factors = [jnp.exp2(peaks[l] - overall) * float(1 << l) for l in range(5)]
        den = sum(factors[l] * expand(tot[where[l], :], l) for l in range(5))
        num = sum(factors[l] * expand(sm[where[l], :], l) for l in range(5))
        inverse = 1.0 / den
        out = num * inverse
        oa[pl.ds(BLOCK * b, BLOCK), :] = out.astype(BF16)
        cot = go[pl.ds(BLOCK * b, BLOCK), :]
        delta = jnp.broadcast_to(jnp.sum(cot * out, axis=1, keepdims=True), (BLOCK, BLOCK))
        cot, delta = cot * inverse, delta * inverse
        for l in range(5):
            gg[where[l], :] = group(factors[l] * cot, l)
            dd[where[l], :] = group(factors[l] * delta, l)

    def backward(level, c=0):
        r0, n, ref, k0, m, _ = unit(level, c)
        rows, keys = pl.ds(r0, n), pl.ds(k0, m)
        gb = gg[rows, :].astype(BF16)
        eb = ee[rows, :m]
        shift = jnp.concatenate([dd[rows, :]] * (m // BLOCK), axis=1)
        ds = eb.astype(F32) * (dot(gb, ref[keys, BLOCK:], NT) - shift)
        ds = (ds * scale).astype(BF16)
        dq[rows, :] = dot(ds, ref[keys, :BLOCK])
        return dot(ds, qs[rows, :], TN), dot(eb, gb, TN)

    def sides(parts):
        return ((parts[0], pl.ds(0, BLOCK)), (parts[1], pl.ds(BLOCK, BLOCK)))

    def start_back(level):
        for entry in peers:
            if entry[0] == level:
                when(entry[6], lambda: back_copy(entry).start())

    for level in (4, 3):
        for part, lanes in sides(backward(level)):
            outbox[level][:, lanes] = part.astype(BF16)
        start_back(level)
    for part, lanes in sides(backward(1, 0)):
        acc1[pl.ds(0, 384), lanes] = part
    for part, lanes in sides(backward(1, 1)):
        edge[pl.ds(0, 64), lanes] = part[:64]
        bk1[pl.ds(64, 64), lanes] = part[64:128].astype(BF16)
        bk1[pl.ds(128, 256), lanes] = (part[128:] + acc1[pl.ds(0, 256), lanes]).astype(BF16)
        bk1[pl.ds(384, 64), lanes] = acc1[pl.ds(256, 64), lanes].astype(BF16)
        edge[pl.ds(64, 64), lanes] = acc1[pl.ds(320, 64), lanes]
    start_back(1)
    for part, lanes in sides(backward(0, 0)):
        fold = 0.5 * expand(edge[pl.ds(0, 64), lanes], 1)
        bk0[pl.ds(0, 128), lanes] = (part[:128] + fold).astype(BF16)
        acc0[pl.ds(0, 256), lanes] = part[128:]
    for part, lanes in sides(backward(0, 3)):
        acc0[pl.ds(256, 256), lanes] = part[:256]
        fold = 0.5 * expand(edge[pl.ds(64, 64), lanes], 1)
        bk0[pl.ds(128, 128), lanes] = (part[256:] + fold).astype(BF16)
    start_back(0)
    for level in (2,):
        for part, lanes in sides(backward(level)):
            outbox[level][:, lanes] = part.astype(BF16)
        start_back(level)
    for part, lanes in sides(backward(0, 1)):
        acc0[pl.ds(0, 384), lanes] += part
    for part, lanes in sides(backward(0, 2)):
        acc0[pl.ds(128, 384), lanes] += part

    chunk = 4 * BLOCK // head_count

    def out_copy(index, src, dst, j):
        to = lax.rem(h + j, head_count)
        n = dst.shape[0]
        return pltpu.make_async_remote_copy(
            src_ref=src.at[pl.ds(pl.multiple_of(to * n, n), n), :],
            dst_ref=dst.at[:, pl.ds(pl.multiple_of(h * BLOCK, BLOCK), BLOCK)],
            send_sem=out_send.at[index, to],
            recv_sem=out_recv.at[index, h],
            device_id={"head": to},
            device_id_type=MESH,
        )

    def out_arrival(index, dst, j):
        frm = lax.rem(h + j, head_count)
        here = dst.at[:, pl.ds(pl.multiple_of(frm * BLOCK, BLOCK), BLOCK)]
        pltpu.make_async_remote_copy(
            src_ref=here, dst_ref=here,
            send_sem=out_send.at[index, frm], recv_sem=out_recv.at[index, frm],
            device_id={"head": h}, device_id_type=MESH,
        ).wait_recv()

    def keep(src, dst):
        dst[:, pl.ds(pl.multiple_of(h * BLOCK, BLOCK), BLOCK)] = src[
            pl.ds(pl.multiple_of(h * dst.shape[0], dst.shape[0]), dst.shape[0]), :
        ]

    pl.semaphore_wait(core_sem, 1)
    for b in range(4):
        total = dq[pl.ds(OFF[4] + 8 * b, 8), :]
        for l in (3, 2, 1, 0):
            total = dq[pl.ds(OFF[l] + (BLOCK >> l) * b, BLOCK >> l), :] + 0.5 * expand(total, 1)
        oq[pl.ds(BLOCK * b, BLOCK), :] = dot(unperm, total.astype(BF16)).astype(BF16)
    for j in FAR_FIRST:
        out_copy(0, oq, gq_ref, j).start()
    keep(oq, gq_ref)
    for b in range(4):
        rows = pl.ds(BLOCK * b, BLOCK)
        att_ref[rows, :] = dot(unperm, oa[rows, :]).astype(BF16)

    for entry in at_level(4) + at_level(3):
        when(entry[4], lambda: back_arrival(entry))
    sum4 = rx4[pl.ds(0, BLOCK), :].astype(F32) + rx4[pl.ds(BLOCK, BLOCK), :].astype(F32)
    panel[...] = 0.5 * expand(sum4, 1)
    near_rows = pl.ds(pl.multiple_of(right * BLOCK, BLOCK), BLOCK)
    far_rows = pl.ds(pl.multiple_of((1 - right) * BLOCK, BLOCK), BLOCK)
    panel[near_rows, :] += rx3[pl.ds(0, BLOCK), :].astype(F32) + rx3[pl.ds(BLOCK, BLOCK), :].astype(F32)
    panel[far_rows, :] += rx3[pl.ds(2 * BLOCK, BLOCK), :].astype(F32)
    cots[...] = panel[...].astype(BF16)
    for d in (2, 1, 3):
        piece_back(d).start()

    for entry in at_level(1) + at_level(0):
        when(entry[4], lambda: back_arrival(entry))
    for b in range(4):
        sum1 = jnp.zeros((64, WIDE), F32)
        if b > 0:
            sum1 = sum1 + rx1[pl.ds(64 * (3 - b), 64), :].astype(F32)
        if b < 3:
            sum1 = sum1 + rx1[pl.ds(192 + 64 * (2 - b), 64), :].astype(F32)
        total = acc0[pl.ds(BLOCK * b, BLOCK), :] + 0.5 * expand(sum1, 1)
        if b == 0:
            total = total + rx0[pl.ds(0, BLOCK), :].astype(F32)
        if b == 3:
            total = total + rx0[pl.ds(BLOCK, BLOCK), :].astype(F32)
        done = dot(unperm, total.astype(BF16)).astype(BF16)
        ok[pl.ds(BLOCK * b, BLOCK), :] = done[:, :BLOCK]
        ov[pl.ds(BLOCK * b, BLOCK), :] = done[:, BLOCK:]
    for j in FAR_FIRST:
        out_copy(1, ok, gk_ref, j).start()
        out_copy(2, ov, gv_ref, j).start()
    keep(ok, gk_ref)
    keep(ov, gv_ref)

    for entry in at_level(2):
        when(entry[4], lambda: back_arrival(entry))
    sum3 = panel[pl.ds(pl.multiple_of(x * 64, 64), 64), :]
    for d in (1, 2, 3):
        row_arrival(parts, back_send, back_recv, d)
        frm = lax.rem(x + d, 4)
        sum3 = sum3 + parts[pl.ds(pl.multiple_of(frm * 64, 64), 64), :].astype(F32)
    sum2 = sum(rx2[pl.ds(128 * i, 128), :].astype(F32) for i in range(3)) + 0.5 * expand(sum3, 1)
    r64, c64 = row[:64, :64], col[:64, :64]
    nth = 8 * (r64 >> 4) + (r64 & 7)
    pick = jnp.where(
        c64 == 32 * ((r64 >> 3) & 1) + 8 * (nth & 3) + (nth >> 2), 1.0, 0.0
    ).astype(BF16)
    for b in range(4):
        part = sum2[32 * b : 32 * b + 32]
        part = jnp.concatenate([part[:, :BLOCK], part[:, BLOCK:]], axis=0).astype(BF16)
        oc[pl.ds(64 * b, 64), :] = dot(pick, part).astype(BF16)
    for j in FAR_FIRST:
        out_copy(3, oc, coarse, j).start()
    keep(oc, coarse)
    for entry in peers:
        when(entry[6], lambda: back_copy(entry).wait_send())
    for entry in outward:
        when(entry[4], lambda: forward_copy(entry).wait_send())
    for d in (1, 2, 3):
        piece_back(d).wait_send()
    for index, src, dst in ((0, oq, gq_ref), (1, ok, gk_ref), (2, ov, gv_ref), (3, oc, coarse)):
        for j in range(1, head_count):
            out_copy(index, src, dst, j).wait_send()
            out_arrival(index, dst, j)
    r16, c16 = row[:64, :16], col[:64, :16]
    spread = jnp.where(c16 == 8 * (r16 >> 5) + ((r16 & 31) >> 2), 0.25, 0.0).astype(BF16)
    more = dot(spread, coarse[...])
    gk_ref[...] = (gk_ref[...].astype(F32) + more[:chunk]).astype(BF16)
    gv_ref[...] = (gv_ref[...].astype(F32) + more[chunk:]).astype(BF16)


def write_out(a, b, c, d, a_out, b_out, c_out, d_out, sem):
    copies = [
        pltpu.make_async_copy(src, dst, sem.at[i])
        for i, (src, dst) in enumerate(((a, a_out), (b, b_out), (c, c_out), (d, d_out)))
    ]
    for copy in copies:
        copy.start()
    for copy in copies:
        copy.wait()


def solution(mesh):
    seq_count, head_count = mesh.shape["seq"], mesh.shape["head"]

    def step(queries, keys, values, grad_out):
        rows, width = queries.shape
        vmem = pl.BlockSpec(memory_space=pltpu.VMEM)
        grad = jax.ShapeDtypeStruct((rows // head_count, width * head_count), BF16)

        def wide(n, dtype=BF16):
            return pltpu.VMEM((n, WIDE), dtype)

        def stacked(dtype, width=BLOCK):
            return pltpu.VMEM((STACK, width), dtype)

        sems = pltpu.SemaphoreType.DMA
        results = pl.pallas_call(
            functools.partial(kernel, seq_count, head_count),
            out_shape=(jax.ShapeDtypeStruct((rows, width), BF16), grad, grad, grad),
            in_specs=[pl.BlockSpec(memory_space=pltpu.HBM)] * 4,
            out_specs=(vmem,) * 4,
            scratch_shapes=[
                wide(768), wide(256), wide(128), wide(64), wide(32),
                wide(512), wide(384), wide(384), wide(256),
                stacked(BF16), pltpu.VMEM((rows, width), F32), stacked(BF16, 384),
                stacked(F32), stacked(F32), stacked(F32), stacked(F32), stacked(F32), stacked(F32),
                wide(512, F32), wide(384, F32), wide(128, F32),
                wide(256), wide(512), wide(384), wide(384), wide(256),
                wide(256), wide(384), wide(384), wide(384), wide(256),
                wide(256, F32), wide(256), wide(256),
                *[pltpu.VMEM((rows, width), BF16) for _ in range(4)],
                pltpu.VMEM((256, BLOCK), BF16), pltpu.VMEM((16, width * head_count), BF16),
                *[pltpu.VMEM((rows, width), BF16) for _ in range(4)],
                sems((4,)),
                sems((OUT_SLOTS,)), sems((OUT_SLOTS,)), sems((SLOTS,)), sems((SLOTS,)),
                sems((4, head_count)), sems((4, head_count)),
                *[pltpu.SemaphoreType.REGULAR for _ in range(3)],
            ],
            compiler_params=pltpu.CompilerParams(
                collective_id=0, has_side_effects=True, vmem_limit_bytes=56000000
            ),
        )(queries, keys, values, grad_out)
        return pl.pallas_call(
            write_out,
            out_shape=tuple(jax.ShapeDtypeStruct(r.shape, r.dtype) for r in results),
            in_specs=[vmem] * 4,
            out_specs=(pl.BlockSpec(memory_space=pltpu.HBM),) * 4,
            scratch_shapes=[sems((4,))],
            compiler_params=pltpu.CompilerParams(vmem_limit_bytes=1024 * 1024),
        )(*results)

    return jax.shard_map(
        step,
        mesh=mesh,
        in_specs=(P("seq", "head"),) * 4,
        out_specs=(P("seq", "head"),) + (P(("seq", "head"), None),) * 3,
        check_vma=False,
    )
```
